256 devices in a mesh: ctx: 64 (over z, x, core), ch: 4 (over y).
Axes of the slice: x: 4, y: 4, z: 8, core: 2. Of those that a mesh axis runs over, the one named last changes fastest.
Arguments:
- streams: bfloat16 [3, 8192, 16384], P(None, ('ch', 'ctx')), may hold values from -6 to 6
- short_taps: float32 [3, 512, 7], P(None, 'ch'), may hold values from -3 to 3
- pole_rates: float32 [512, 16], P('ch'), may hold values from 3.0517578e-06 to 0.2, as said below
- residues: float32 [512, 16], P('ch'), may hold values from -0.6 to 0.6
- skip: float32 [8192], P('ch'), may hold values from -1 to 1
- gain: float32 [8192], P('ch'), may hold values from 0.1 to 1.9
Outputs:
- normed: bfloat16 [8192, 16384], P('ch', 'ctx')
The draws below stay inside these ranges and needn't reach their ends.
Inputs may be any that keep to these rules, and one draw needn't show every extreme that they name: `pole_rates`: decay rates, all positive.
All inputs are finite; a program needn't handle non-finite values.
Results may differ from the reference program's by a relative error of at most 0.001.
Values may be sent and summed in bfloat16 or wider, within the bound.
No kernel may reach another device: no remote copies, remote signals or barrier semaphores. Data moves between devices by JAX's collectives and lax.ppermute only.
A program may use at most 128 MiB of HBM per device.

```python
import math
import jax
import jax.numpy as jnp
from jax import lax

D = 8192
GROUPS = 512
POLES = 16
SHORT = 7
BLOCK = 128
SEQ = 16384


def pole_law(key):
    keys = jax.random.split(jax.random.fold_in(key, 7), 3)
    shape_here = (GROUPS, POLES)
    slow_rates = jnp.exp(jax.random.uniform(keys[0], shape_here, jnp.float32, math.log(0.05 / SEQ), math.log(1.5 / SEQ)))
    fast_rates = jnp.exp(jax.random.uniform(keys[1], shape_here, jnp.float32, math.log(0.02), math.log(0.2)))
    share = 0.5
    keep_slow = jax.random.uniform(keys[2], shape_here, jnp.float32) < share
    return jnp.where(keep_slow, slow_rates, fast_rates)


def draw_pole_rates(key, part):
    return pole_law(key)


def draw_residues(key, part):
    rates_drawn = pole_law(key)
    residue_key = jax.random.fold_in(key, 13)
    base_values = jnp.clip(jax.random.normal(residue_key, (GROUPS, POLES), jnp.float32), -4.0, 4.0)
    return base_values * jnp.sqrt(2.0 * rates_drawn + 2.0 / SEQ) * 0.2


def levels(own_key, extent, pieces, low, top_value):
    level = 1.0
    for axis_at, blocks in pieces:
        steps = jax.random.uniform(jax.random.fold_in(jax.random.fold_in(own_key, 6), axis_at), (blocks,), jnp.float32, low / len(pieces), top_value / len(pieces))
        level = level * jnp.repeat(jnp.exp(steps), extent[axis_at] // blocks).reshape((-1,) + (1,) * (len(extent) - 1 - axis_at))
    return level


def scatter_about(rng, dims, scale, limit, cuts=(), held_as=jnp.bfloat16):
    level = levels(rng, dims, cuts, -0.22, 0.18) if cuts else 1.0
    result = jax.random.normal(rng, dims, jnp.float32) * scale * level
    return jnp.minimum(jnp.maximum(result, -limit), limit).astype(held_as)


def setup_inputs(seed: int = 0) -> dict:
    streams_of = jax.random.split(jax.random.key(seed), 7)
    streams = scatter_about(streams_of[0], (3, D, SEQ), 1.0, 6.0, ((1, 256),))
    short_taps = scatter_about(streams_of[1], (3, GROUPS, SHORT), 0.4, 3.0, ((1, 4),), jnp.float32)
    pole_rates = draw_pole_rates(jax.random.fold_in(streams_of[6], 71), 0)
    residues = draw_residues(jax.random.fold_in(streams_of[6], 71), 0)
    skip = jnp.clip(jax.random.uniform(streams_of[4], (D,), jnp.float32, -1.0, 1.0) * levels(streams_of[4], (D,), ((0, 4),), -0.4, 0.0), -1.0, 1.0)
    gain = jnp.clip(1.0 + 0.18 * jax.random.normal(streams_of[5], (D,), jnp.float32), 0.1, 1.9)
    return {"streams": streams, "short_taps": short_taps, "pole_rates": pole_rates, "residues": residues, "skip": skip, "gain": gain}


HIGHEST_PRECISION = lax.Precision.HIGHEST

def short_filter(extended, short_taps, groups, length):
    reach_back = short_taps.shape[2] - 1
    channels = extended.shape[1]
    shaped = extended.reshape(3, groups, channels // groups, extended.shape[2])
    summed = jnp.zeros((3, groups, channels // groups, length), jnp.float32)
    for offset in range(short_taps.shape[2]):
        window = shaped[:, :, :, reach_back - offset:reach_back - offset + length].astype(jnp.float32)
        summed = summed + short_taps[:, :, offset][:, :, None, None] * window
    return summed

def kernel_table(pole_rates, residues, block):
    row_index = jnp.arange(block, dtype=jnp.int32)[:, None]
    col_index = jnp.arange(block, dtype=jnp.int32)[None, :]
    lag_flat = (row_index - col_index).reshape(-1)
    step_values = jnp.arange(block, dtype=jnp.int32).astype(jnp.float32)
    modal_row = jnp.einsum('gp,gpl->gl', residues, jnp.exp(-pole_rates[:, :, None] * step_values), precision=HIGHEST_PRECISION)
    picker = (jnp.arange(block, dtype=jnp.int32)[:, None] == lag_flat[None, :]).astype(jnp.float32)
    table = jnp.dot(modal_row, picker, precision=HIGHEST_PRECISION, preferred_element_type=jnp.float32)
    return table.reshape(modal_row.shape[0], block, block)

def compose(earlier, later_pair):
    return (earlier[0] * later_pair[0], later_pair[0] * earlier[1] + later_pair[1])

def block_terms(product, kernel, pole_rates, block):
    groups, group_width, length = product.shape
    block_count = length // block
    current = product.reshape(groups, group_width, block_count, block)
    inner_part = jnp.einsum('gsnk,gik->gsni', current, kernel, precision=HIGHEST_PRECISION)
    reverse_steps = (block - 1 - jnp.arange(block, dtype=jnp.int32)).astype(jnp.float32)
    backward = jnp.exp(-pole_rates[:, :, None] * reverse_steps)
    end_states = jnp.einsum('gsnk,gpk->gsnp', current, backward, precision=HIGHEST_PRECISION)
    decays = jnp.broadcast_to(jnp.exp(-pole_rates * block)[:, None, None, :], end_states.shape)
    lifted, prefix = lax.associative_scan(compose, (decays, end_states), axis=2)
    return (inner_part, prefix)

def finish_terms(inner_part, prefix, state_in, pole_rates, residues, block):
    groups, group_width, block_count, block_size = inner_part.shape
    counts = jnp.arange(1, block_count + 1, dtype=jnp.int32).astype(jnp.float32) * block
    powers = jnp.exp(-pole_rates[:, None, :] * counts[None, :, None])
    after_block = prefix + powers[:, None, :, :] * state_in[:, :, None, :]
    starts = jnp.concatenate([state_in[:, :, None, :], after_block[:, :, :-1, :]], axis=2)
    lift_steps = jnp.arange(1, block + 1, dtype=jnp.int32).astype(jnp.float32)
    lift_table = residues[:, :, None] * jnp.exp(-pole_rates[:, :, None] * lift_steps)
    carried = jnp.einsum('gsnp,gpi->gsni', starts, lift_table, precision=HIGHEST_PRECISION)
    return (inner_part + carried).reshape(groups, group_width, block_count * block)

def reference(streams, short_taps, pole_rates, residues, skip, gain):
    group_size = D // GROUPS
    length = streams.shape[2]

    def one_group(group_index):
        group_rows = lax.dynamic_slice_in_dim(streams, group_index * group_size, group_size, 1)
        taps_here = lax.dynamic_slice_in_dim(short_taps, group_index, 1, 1)
        rates_here = lax.dynamic_slice_in_dim(pole_rates, group_index, 1, 0)
        residue_here = lax.dynamic_slice_in_dim(residues, group_index, 1, 0)
        skip_here = lax.dynamic_slice_in_dim(skip, group_index * group_size, group_size, 0)
        extended = jnp.concatenate([jnp.zeros((3, group_size, SHORT - 1), streams.dtype), group_rows], axis=2)
        filtered = short_filter(extended, taps_here, 1, length)
        product = filtered[1] * filtered[2]
        kernel = kernel_table(rates_here, residue_here, BLOCK)
        inner_part, prefix = block_terms(product, kernel, rates_here, BLOCK)
        state_zero = jnp.zeros((1, group_size, POLES), jnp.float32)
        convolved = finish_terms(inner_part, prefix, state_zero, rates_here, residue_here, BLOCK)
        gated_value = filtered[0] * (convolved + skip_here[None, :, None] * product)
        return gated_value[0]
    gated_value = lax.map(one_group, jnp.arange(GROUPS, dtype=jnp.int32)).reshape(D, length)
    mean_square = lax.optimization_barrier(jnp.mean(gated_value * gated_value, axis=0))
    return (gated_value * gain[:, None] * lax.rsqrt(mean_square + 1e-05)[None, :]).astype(jnp.bfloat16)
```

```python
import jax
import jax.numpy as jnp
from jax import lax
from jax.experimental import pallas as pl
from jax.experimental.pallas import tpu as pltpu
from jax.sharding import Mesh
from jax.sharding import PartitionSpec as P

D = 8192
SHORT = 7
BLOCK = 128
WIDTH = 16
CTX = ("ctx_0", "ctx_1", "ctx_2")
CH_CTX = ("ch", "ctx_0", "ctx_1", "ctx_2")
CHUNK = 32


def split(value):
    high = value.astype(jnp.bfloat16)
    low = (value - high.astype(jnp.float32)).astype(jnp.bfloat16)
    return high, low


def column_of(row):
    width = row.shape[1]
    rows = lax.broadcasted_iota(jnp.int32, (width, width), 0)
    cols = lax.broadcasted_iota(jnp.int32, (width, width), 1)
    return jnp.sum(jnp.where(rows == cols, row, 0.0), axis=1, keepdims=True)


def toeplitz(row, rows):
    spread = jnp.broadcast_to(row, (rows, row.shape[1]))
    return pltpu.roll(spread, 0, 1, stride=1, stride_axis=0)


def mix_kernel(
    place, streams, short_taps, rates, residues, skip, gated_out, square_out,
    taps_w, conv_w, lift_w, first, direct, ends, starts, squares,
):
    blocks = streams.shape[2] // BLOCK
    group = place[0] * pl.num_programs(0) + pl.program_id(0)
    rate = column_of(rates[pl.ds(group, 1), :])
    residue = column_of(residues[pl.ds(group, 1), :])
    skip_column = column_of(skip[pl.ds(group, 1), :])
    zero = jnp.zeros((BLOCK, BLOCK), jnp.bfloat16)

    for m in range(3):
        taps = short_taps[m, pl.ds(group, 1), :]
        row = jnp.concatenate([taps, jnp.zeros((1, 2 * BLOCK - SHORT), jnp.float32)], axis=1)
        high, low = split(toeplitz(row, 2 * BLOCK)[:, BLOCK:])
        taps_w[m] = jnp.concatenate([high, low], axis=1)

    steps = lax.broadcasted_iota(jnp.int32, (WIDTH, BLOCK), 1).astype(jnp.float32)
    kernel_row = jnp.sum(residue * jnp.exp(-rate * steps), axis=0, keepdims=True)
    lags = toeplitz(kernel_row, BLOCK)
    at_row = lax.broadcasted_iota(jnp.int32, (BLOCK, BLOCK), 0)
    at_col = lax.broadcasted_iota(jnp.int32, (BLOCK, BLOCK), 1)
    high, low = split(jnp.where(at_col >= at_row, lags, 0.0))
    conv_w[:, : 2 * BLOCK] = jnp.concatenate(
        [jnp.concatenate([high, low], axis=1), jnp.concatenate([high, zero], axis=1)], axis=0
    )
    backward = jnp.exp(-rate * (BLOCK - 1 - steps))
    thrice = jnp.concatenate(
        [backward, backward, backward, jnp.zeros((BLOCK - 3 * WIDTH, BLOCK), jnp.float32)], axis=0
    ).T
    high, low = split(thrice)
    conv_w[:, 2 * BLOCK :] = jnp.concatenate(
        [jnp.concatenate([high, low], axis=1), jnp.concatenate([high, zero], axis=1)], axis=0
    )
    high, low = split(residue * jnp.exp(-rate * (steps + 1.0)))
    lift_w[...] = jnp.concatenate(
        [high, high, low, jnp.zeros((BLOCK - 3 * WIDTH, BLOCK), jnp.bfloat16)], axis=0
    )

    skip_rows = jnp.broadcast_to(
        skip_column[None], (CHUNK, WIDTH, BLOCK)
    ).reshape(CHUNK * WIDTH, BLOCK)
    for chunk in range(blocks // CHUNK):
        span = pl.ds(chunk * CHUNK * WIDTH, CHUNK * WIDTH)
        filtered = []
        for m in range(3):
            pieces = []
            for n in range(chunk * CHUNK, (chunk + 1) * CHUNK):
                if n == 0:
                    here = streams[m, :, :BLOCK]
                    pieces.append(jnp.concatenate([jnp.zeros_like(here), here], axis=1))
                else:
                    pieces.append(streams[m, :, (n - 1) * BLOCK : (n + 1) * BLOCK])
            both = jnp.dot(
                jnp.concatenate(pieces, axis=0), taps_w[m], preferred_element_type=jnp.float32
            )
            filtered.append(both[:, :BLOCK] + both[:, BLOCK:])
        product = filtered[1] * filtered[2]
        high, low = split(product)
        terms = jnp.dot(
            jnp.concatenate([high, low], axis=1), conv_w[...], preferred_element_type=jnp.float32
        )
        first[span, :] = filtered[0]
        direct[span, :] = (terms[:, :BLOCK] + terms[:, BLOCK : 2 * BLOCK]) + skip_rows * product
        ends[span, :] = terms[:, 2 * BLOCK : 3 * BLOCK] + terms[:, 3 * BLOCK :]

    decay_row = jnp.exp(-rates[pl.ds(group, 1), :] * float(BLOCK))
    decay = jnp.broadcast_to(
        jnp.concatenate(
            [decay_row, decay_row, decay_row, jnp.zeros((1, BLOCK - 3 * WIDTH), jnp.float32)],
            axis=1,
        ),
        (WIDTH, BLOCK),
    )
    lane = lax.broadcasted_iota(jnp.int32, (WIDTH, BLOCK), 1)
    takes_low = (lane >= WIDTH) & (lane < 2 * WIDTH)
    state = jnp.zeros((WIDTH, BLOCK), jnp.float32)
    for n in range(blocks):
        high = state.astype(jnp.bfloat16).astype(jnp.float32)
        starts[pl.ds(n * WIDTH, WIDTH), :] = jnp.where(takes_low, state - high, high).astype(
            jnp.bfloat16
        )
        state = decay * state + ends[pl.ds(n * WIDTH, WIDTH), :]

    for chunk in range(blocks // CHUNK):
        span = pl.ds(chunk * CHUNK * WIDTH, CHUNK * WIDTH)
        carried = jnp.dot(starts[span, :], lift_w[...], preferred_element_type=jnp.float32)
        gated = first[span, :] * (direct[span, :] + carried)
        for k in range(CHUNK):
            n = chunk * CHUNK + k
            gated_out[n // 2, :, (n % 2) * BLOCK : (n % 2 + 1) * BLOCK] = gated[
                k * WIDTH : (k + 1) * WIDTH
            ]
        squared = (gated * gated).reshape(CHUNK, 2, 8, BLOCK)
        squared = squared[:, 0] + squared[:, 1]
        rows = pl.ds(chunk * CHUNK, CHUNK)

        @pl.when(pl.program_id(0) == 0)
        def _():
            squares[rows] = squared

        @pl.when(pl.program_id(0) != 0)
        def _():
            squares[rows] = squares[rows] + squared

    @pl.when(pl.program_id(0) == pl.num_programs(0) - 1)
    def _():
        square_out[...] = jnp.sum(squares[...], axis=1)


def mix(place, streams, short_taps, rates, residues, skip):
    channels, length = streams.shape[1:]
    blocks = length // BLOCK
    rows = blocks * WIDTH
    whole = lambda array: pl.BlockSpec(array.shape, lambda g, place: (0,) * array.ndim)
    return pl.pallas_call(
        mix_kernel,
        name="mix",
        grid_spec=pltpu.PrefetchScalarGridSpec(
            num_scalar_prefetch=1,
            grid=(channels // WIDTH,),
            in_specs=[
                pl.BlockSpec((3, WIDTH, length), lambda g, place: (0, g, 0)),
                whole(short_taps),
                whole(rates),
                whole(residues),
                whole(skip),
            ],
            out_specs=[
                pl.BlockSpec((blocks // 2, WIDTH, 2 * BLOCK), lambda g, place: (0, g, 0)),
                pl.BlockSpec((blocks, BLOCK), lambda g, place: (0, 0)),
            ],
            scratch_shapes=[
                pltpu.VMEM((3, 2 * BLOCK, 2 * BLOCK), jnp.bfloat16),
                pltpu.VMEM((2 * BLOCK, 4 * BLOCK), jnp.bfloat16),
                pltpu.VMEM((BLOCK, BLOCK), jnp.bfloat16),
                pltpu.VMEM((rows, BLOCK), jnp.float32),
                pltpu.VMEM((rows, BLOCK), jnp.float32),
                pltpu.VMEM((rows, BLOCK), jnp.float32),
                pltpu.VMEM((rows, BLOCK), jnp.bfloat16),
                pltpu.VMEM((blocks, 8, BLOCK), jnp.float32),
            ],
        ),
        out_shape=[
            jax.ShapeDtypeStruct((blocks // 2, channels, 2 * BLOCK), jnp.float32),
            jax.ShapeDtypeStruct((blocks, BLOCK), jnp.float32),
        ],
        compiler_params=pltpu.CompilerParams(dimension_semantics=("arbitrary",)),
    )(place, streams, short_taps, rates, residues, skip)


def shards(streams, short_taps, pole_rates, residues, skip, gain):
    channels = streams.shape[1]
    groups = pole_rates.shape[0]
    place = lax.axis_index(CTX)
    gated, squares = mix(
        place.reshape(1), streams, short_taps, pole_rates, residues, skip.reshape(groups, WIDTH)
    )
    mean_square = lax.psum(squares, CH_CTX) / D
    scale = lax.rsqrt(mean_square + 1e-05).reshape(gated.shape[0], 1, gated.shape[2])
    own_gain = lax.dynamic_slice(gain, (place * channels,), (channels,))
    normed = (gated * own_gain[None, :, None] * scale).astype(jnp.bfloat16)
    moved = lax.all_to_all(normed, CTX, split_axis=0, concat_axis=0, tiled=True)
    return moved.reshape(moved.shape[0] * channels, moved.shape[2])


def solution(mesh):
    torus = Mesh(mesh.devices.reshape(8, 4, 2, mesh.shape["ch"]), ("ctx_0", "ctx_1", "ctx_2", "ch"))
    in_specs = (
        P(None, CH_CTX, None),
        P(None, "ch", None),
        P("ch", None),
        P("ch", None),
        P("ch"),
        P("ch"),
    )
    out_specs = P("ch", CTX)
    return jax.shard_map(
        shards, mesh=torus, in_specs=in_specs, out_specs=out_specs, check_vma=False
    )
```

```python
import jax
import jax.numpy as jnp
from jax import lax
from jax.experimental import pallas as pl
from jax.experimental.pallas import tpu as pltpu
from jax.sharding import Mesh
from jax.sharding import PartitionSpec as P

D = 8192
SHORT = 7
BLOCK = 128
WIDTH = 16
CTX = ("ctx_0", "ctx_1", "ctx_2")
CH_CTX = ("ch", "ctx_0", "ctx_1", "ctx_2")
CHUNK = 32
TOP = 32768.0
TINY = 1e-37


def split(value):
    high = value.astype(jnp.bfloat16)
    low = (value - high.astype(jnp.float32)).astype(jnp.bfloat16)
    return high, low


def picked_column(array, first, step):
    rows = lax.broadcasted_iota(jnp.int32, (array.shape[0], BLOCK), 0)
    cols = lax.broadcasted_iota(jnp.int32, (array.shape[0], BLOCK), 1)
    return jnp.sum(jnp.where(cols == first + step * rows, array, 0.0), axis=1, keepdims=True)


def row_of(column, lanes):
    rows = lax.broadcasted_iota(jnp.int32, (column.shape[0], lanes), 0)
    cols = lax.broadcasted_iota(jnp.int32, (column.shape[0], lanes), 1)
    return jnp.sum(jnp.where(rows == cols, column, 0.0), axis=0, keepdims=True)


def channel_column(ref, group):
    per_row = BLOCK // WIDTH
    row = jnp.broadcast_to(ref[pl.ds(group // per_row, 1), :], (WIDTH, BLOCK))
    return picked_column(row, (group % per_row) * WIDTH, 1)


def toeplitz(row, rows):
    spread = jnp.broadcast_to(row, (rows, row.shape[1]))
    return pltpu.roll(spread, 0, 1, stride=1, stride_axis=0)


def mix_kernel(
    place, streams, short_taps, rates, residues, skip, gain, gated_out, side_out,
    taps_w, conv_w, lift_w, first, direct, ends, starts, squares, peaks,
):
    blocks = streams.shape[2] // BLOCK
    group = place[0] * pl.num_programs(0) + pl.program_id(0)
    rate = picked_column(rates[...], group, 0)
    residue = picked_column(residues[...], group, 0)
    skip_column = channel_column(skip, group)
    gain_column = channel_column(gain, group)
    zero = jnp.zeros((BLOCK, BLOCK), jnp.bfloat16)

    for m in range(3):
        row = row_of(picked_column(short_taps[m], group, 0), 2 * BLOCK)
        high, low = split(toeplitz(row, 2 * BLOCK)[:, BLOCK:])
        taps_w[m] = jnp.concatenate([high, low], axis=1)

    steps = lax.broadcasted_iota(jnp.int32, (WIDTH, BLOCK), 1).astype(jnp.float32)
    kernel_row = jnp.sum(residue * jnp.exp(-rate * steps), axis=0, keepdims=True)
    lags = toeplitz(kernel_row, BLOCK)
    at_row = lax.broadcasted_iota(jnp.int32, (BLOCK, BLOCK), 0)
    at_col = lax.broadcasted_iota(jnp.int32, (BLOCK, BLOCK), 1)
    high, low = split(jnp.where(at_col >= at_row, lags, 0.0))
    conv_w[:, : 2 * BLOCK] = jnp.concatenate(
        [jnp.concatenate([high, low], axis=1), jnp.concatenate([high, zero], axis=1)], axis=0
    )
    backward = jnp.exp(-rate * (BLOCK - 1 - steps))
    thrice = jnp.concatenate(
        [backward, backward, backward, jnp.zeros((BLOCK - 3 * WIDTH, BLOCK), jnp.float32)], axis=0
    ).T
    high, low = split(thrice)
    conv_w[:, 2 * BLOCK :] = jnp.concatenate(
        [jnp.concatenate([high, low], axis=1), jnp.concatenate([high, zero], axis=1)], axis=0
    )
    high, low = split(residue * jnp.exp(-rate * (steps + 1.0)))
    lift_w[...] = jnp.concatenate(
        [high, high, low, jnp.zeros((BLOCK - 3 * WIDTH, BLOCK), jnp.bfloat16)], axis=0
    )

    skip_rows = jnp.broadcast_to(
        skip_column[None], (CHUNK, WIDTH, BLOCK)
    ).reshape(CHUNK * WIDTH, BLOCK)
    gain_rows = jnp.broadcast_to(
        gain_column[None], (CHUNK, WIDTH, BLOCK)
    ).reshape(CHUNK * WIDTH, BLOCK)
    for chunk in range(blocks // CHUNK):
        span = pl.ds(chunk * CHUNK * WIDTH, CHUNK * WIDTH)
        filtered = []
        for m in range(3):
            pieces = []
            for n in range(chunk * CHUNK, (chunk + 1) * CHUNK):
                if n == 0:
                    here = streams[m, :, :BLOCK]
                    pieces.append(jnp.concatenate([jnp.zeros_like(here), here], axis=1))
                else:
                    pieces.append(streams[m, :, (n - 1) * BLOCK : (n + 1) * BLOCK])
            both = jnp.dot(
                jnp.concatenate(pieces, axis=0), taps_w[m], preferred_element_type=jnp.float32
            )
            filtered.append(both[:, :BLOCK] + both[:, BLOCK:])
        product = filtered[1] * filtered[2]
        high, low = split(product)
        terms = jnp.dot(
            jnp.concatenate([high, low], axis=1), conv_w[...], preferred_element_type=jnp.float32
        )
        first[span, :] = filtered[0]
        direct[span, :] = (terms[:, :BLOCK] + terms[:, BLOCK : 2 * BLOCK]) + skip_rows * product
        ends[span, :] = terms[:, 2 * BLOCK : 3 * BLOCK] + terms[:, 3 * BLOCK :]

    decay_column = jnp.exp(-rate * float(BLOCK))
    decay = jnp.broadcast_to(
        row_of(jnp.concatenate([decay_column] * 3, axis=0), BLOCK), (WIDTH, BLOCK)
    )
    lane = lax.broadcasted_iota(jnp.int32, (WIDTH, BLOCK), 1)
    takes_low = (lane >= WIDTH) & (lane < 2 * WIDTH)
    state = jnp.zeros((WIDTH, BLOCK), jnp.float32)
    for n in range(blocks):
        high = state.astype(jnp.bfloat16).astype(jnp.float32)
        starts[pl.ds(n * WIDTH, WIDTH), :] = jnp.where(takes_low, state - high, high).astype(
            jnp.bfloat16
        )
        state = decay * state + ends[pl.ds(n * WIDTH, WIDTH), :]

    for chunk in range(blocks // CHUNK):
        span = pl.ds(chunk * CHUNK * WIDTH, CHUNK * WIDTH)
        carried = jnp.dot(starts[span, :], lift_w[...], preferred_element_type=jnp.float32)
        gated = first[span, :] * (direct[span, :] + carried)
        gained = gated * gain_rows
        for k in range(CHUNK):
            n = chunk * CHUNK + k
            gated_out[n // 2, :, (n % 2) * BLOCK : (n % 2 + 1) * BLOCK] = gained[
                k * WIDTH : (k + 1) * WIDTH
            ]
        squared = (gated * gated).reshape(CHUNK, 2, 8, BLOCK)
        squared = squared[:, 0] + squared[:, 1]
        size = jnp.abs(gained).reshape(CHUNK, 2, 8, BLOCK)
        size = jnp.maximum(size[:, 0], size[:, 1])
        rows = pl.ds(chunk * CHUNK, CHUNK)

        @pl.when(pl.program_id(0) == 0)
        def _():
            squares[rows] = squared
            peaks[rows] = size

        @pl.when(pl.program_id(0) != 0)
        def _():
            squares[rows] = squares[rows] + squared
            peaks[rows] = jnp.maximum(peaks[rows], size)

    @pl.when(pl.program_id(0) == pl.num_programs(0) - 1)
    def _():
        side_out[0] = jnp.sum(squares[...], axis=1)
        side_out[1] = jnp.maximum(jnp.max(peaks[...], axis=1), TINY)


def mix(place, streams, short_taps, rates, residues, skip, gain):
    channels, length = streams.shape[1:]
    blocks = length // BLOCK
    rows = blocks * WIDTH
    short_taps = short_taps.transpose(0, 2, 1)
    rates = rates.T
    residues = residues.T
    skip = skip.reshape(-1, BLOCK)
    gain = gain.reshape(-1, BLOCK)
    whole = lambda array: pl.BlockSpec(array.shape, lambda g, place: (0,) * array.ndim)
    return pl.pallas_call(
        mix_kernel,
        name="mix",
        grid_spec=pltpu.PrefetchScalarGridSpec(
            num_scalar_prefetch=1,
            grid=(channels // WIDTH,),
            in_specs=[
                pl.BlockSpec((3, WIDTH, length), lambda g, place: (0, g, 0)),
                whole(short_taps),
                whole(rates),
                whole(residues),
                whole(skip),
                whole(gain),
            ],
            out_specs=[
                pl.BlockSpec((blocks // 2, WIDTH, 2 * BLOCK), lambda g, place: (0, g, 0)),
                pl.BlockSpec((2, blocks, BLOCK), lambda g, place: (0, 0, 0)),
            ],
            scratch_shapes=[
                pltpu.VMEM((3, 2 * BLOCK, 2 * BLOCK), jnp.bfloat16),
                pltpu.VMEM((2 * BLOCK, 4 * BLOCK), jnp.bfloat16),
                pltpu.VMEM((BLOCK, BLOCK), jnp.bfloat16),
                pltpu.VMEM((rows, BLOCK), jnp.float32),
                pltpu.VMEM((rows, BLOCK), jnp.float32),
                pltpu.VMEM((rows, BLOCK), jnp.float32),
                pltpu.VMEM((rows, BLOCK), jnp.bfloat16),
                pltpu.VMEM((blocks, 8, BLOCK), jnp.float32),
                pltpu.VMEM((blocks, 8, BLOCK), jnp.float32),
            ],
        ),
        out_shape=[
            jax.ShapeDtypeStruct((blocks // 2, channels, 2 * BLOCK), jnp.float32),
            jax.ShapeDtypeStruct((2, blocks, BLOCK), jnp.float32),
        ],
        compiler_params=pltpu.CompilerParams(dimension_semantics=("arbitrary",)),
    )(place, streams, short_taps, rates, residues, skip, gain)


def from_everyone(array, axis):
    count = lax.axis_size(axis)
    return lax.all_to_all(
        jnp.broadcast_to(array[None], (count, *array.shape)), axis, 0, 0, tiled=True
    )


def shards(streams, short_taps, pole_rates, residues, skip, gain):
    channels = streams.shape[1]
    place = lax.axis_index(CTX)
    gained, side = mix(
        place.reshape(1), streams, short_taps, pole_rates, residues, skip, gain
    )
    owners, channels, length = gained.shape
    side = side.reshape(2, owners, length)
    small = lax.all_to_all(side.transpose(1, 0, 2), CTX, 0, 0, tiled=True)
    own = jnp.sum(small[:, 0], axis=0)
    mean_square = jnp.sum(from_everyone(own, "ch"), axis=0) / D
    scale = small[:, 1] * (TOP**-0.5 * lax.rsqrt(mean_square + 1e-05))[None]
    part = gained * (1.0 / side[1])[:, None, :]
    coded = (part * jnp.abs(part) * TOP).astype(jnp.float16)
    moved = lax.all_to_all(coded, CTX, 0, 0, tiled=True).astype(jnp.float32)
    size = jnp.sqrt(jnp.abs(moved))
    normed = jnp.where(moved < 0, -size, size) * scale[:, None, :]
    return normed.astype(jnp.bfloat16).reshape(owners * channels, length)


def solution(mesh):
    torus = Mesh(mesh.devices.reshape(8, 4, 2, mesh.shape["ch"]), ("ctx_0", "ctx_1", "ctx_2", "ch"))
    in_specs = (
        P(None, CH_CTX, None),
        P(None, "ch", None),
        P("ch", None),
        P("ch", None),
        P("ch"),
        P("ch"),
    )
    out_specs = P("ch", CTX)
    return jax.shard_map(
        shards, mesh=torus, in_specs=in_specs, out_specs=out_specs, check_vma=False
    )
```

```python
import jax
import jax.numpy as jnp
from jax import lax
from jax.experimental import pallas as pl
from jax.experimental.pallas import tpu as pltpu
from jax.sharding import Mesh
from jax.sharding import PartitionSpec as P

D = 8192
SHORT = 7
BLOCK = 128
WIDTH = 16
CTX = ("ctx_0", "ctx_1", "ctx_2")
CH_CTX = ("ch", "ctx_0", "ctx_1", "ctx_2")
CHUNK = 32
TOP = 32768.0
TINY = 1e-37
AT_ONCE = 8


def split(value):
    high = value.astype(jnp.bfloat16)
    low = (value - high.astype(jnp.float32)).astype(jnp.bfloat16)
    return high, low


def picked_column(array, first, step):
    rows = lax.broadcasted_iota(jnp.int32, (array.shape[0], BLOCK), 0)
    cols = lax.broadcasted_iota(jnp.int32, (array.shape[0], BLOCK), 1)
    return jnp.sum(jnp.where(cols == first + step * rows, array, 0.0), axis=1, keepdims=True)


def row_of(column, lanes):
    rows = lax.broadcasted_iota(jnp.int32, (column.shape[0], lanes), 0)
    cols = lax.broadcasted_iota(jnp.int32, (column.shape[0], lanes), 1)
    return jnp.sum(jnp.where(rows == cols, column, 0.0), axis=0, keepdims=True)


def channel_column(ref, group):
    per_row = BLOCK // WIDTH
    row = jnp.broadcast_to(ref[pl.ds(group // per_row, 1), :], (WIDTH, BLOCK))
    return picked_column(row, (group % per_row) * WIDTH, 1)


def toeplitz(row, rows):
    spread = jnp.broadcast_to(row, (rows, row.shape[1]))
    return pltpu.roll(spread, 0, 1, stride=1, stride_axis=0)


def mix_kernel(
    place, streams, short_taps, rates, residues, skip, gain, coded_out,
    taps_w, conv_w, lift_w, first, direct, ends, starts, squares, peaks, gained, rows_in,
):
    blocks = streams.shape[2] // BLOCK
    group = place[0] * pl.num_programs(0) + pl.program_id(0)
    rate = picked_column(rates[...], group, 0)
    residue = picked_column(residues[...], group, 0)
    skip_column = channel_column(skip, group)
    gain_column = channel_column(gain, group)
    zero = jnp.zeros((BLOCK, BLOCK), jnp.bfloat16)

    for m in range(3):
        row = row_of(picked_column(short_taps[m], group, 0), 2 * BLOCK)
        high, low = split(toeplitz(row, 2 * BLOCK)[:, BLOCK:])
        taps_w[m] = jnp.concatenate([high, low], axis=1)

    steps = lax.broadcasted_iota(jnp.int32, (WIDTH, BLOCK), 1).astype(jnp.float32)
    kernel_row = jnp.sum(residue * jnp.exp(-rate * steps), axis=0, keepdims=True)
    lags = toeplitz(kernel_row, BLOCK)
    at_row = lax.broadcasted_iota(jnp.int32, (BLOCK, BLOCK), 0)
    at_col = lax.broadcasted_iota(jnp.int32, (BLOCK, BLOCK), 1)
    high, low = split(jnp.where(at_col >= at_row, lags, 0.0))
    conv_w[:, : 2 * BLOCK] = jnp.concatenate(
        [jnp.concatenate([high, low], axis=1), jnp.concatenate([high, zero], axis=1)], axis=0
    )
    backward = jnp.exp(-rate * (BLOCK - 1 - steps))
    thrice = jnp.concatenate(
        [backward, backward, backward, jnp.zeros((BLOCK - 3 * WIDTH, BLOCK), jnp.float32)], axis=0
    ).T
    high, low = split(thrice)
    conv_w[:, 2 * BLOCK :] = jnp.concatenate(
        [jnp.concatenate([high, low], axis=1), jnp.concatenate([high, zero], axis=1)], axis=0
    )
    high, low = split(residue * jnp.exp(-rate * (steps + 1.0)))
    lift_w[...] = jnp.concatenate(
        [high, high, low, jnp.zeros((BLOCK - 3 * WIDTH, BLOCK), jnp.bfloat16)], axis=0
    )

    skip_rows = jnp.broadcast_to(
        skip_column[None], (CHUNK, WIDTH, BLOCK)
    ).reshape(CHUNK * WIDTH, BLOCK)
    gain_rows = jnp.broadcast_to(
        gain_column[None], (CHUNK, WIDTH, BLOCK)
    ).reshape(CHUNK * WIDTH, BLOCK)
    for chunk in range(blocks // CHUNK):
        span = pl.ds(chunk * CHUNK * WIDTH, CHUNK * WIDTH)
        filtered = []
        for m in range(3):
            pieces = []
            for n in range(chunk * CHUNK, (chunk + 1) * CHUNK):
                if n == 0:
                    here = streams[m, :, :BLOCK]
                    pieces.append(jnp.concatenate([jnp.zeros_like(here), here], axis=1))
                else:
                    pieces.append(streams[m, :, (n - 1) * BLOCK : (n + 1) * BLOCK])
            both = jnp.dot(
                jnp.concatenate(pieces, axis=0), taps_w[m], preferred_element_type=jnp.float32
            )
            filtered.append(both[:, :BLOCK] + both[:, BLOCK:])
        product = filtered[1] * filtered[2]
        high, low = split(product)
        terms = jnp.dot(
            jnp.concatenate([high, low], axis=1), conv_w[...], preferred_element_type=jnp.float32
        )
        first[span, :] = filtered[0]
        direct[span, :] = (terms[:, :BLOCK] + terms[:, BLOCK : 2 * BLOCK]) + skip_rows * product
        ends[span, :] = terms[:, 2 * BLOCK : 3 * BLOCK] + terms[:, 3 * BLOCK :]

    decay_column = jnp.exp(-rate * float(BLOCK))
    decay = jnp.broadcast_to(
        row_of(jnp.concatenate([decay_column] * 3, axis=0), BLOCK), (WIDTH, BLOCK)
    )
    lane = lax.broadcasted_iota(jnp.int32, (WIDTH, BLOCK), 1)
    takes_low = (lane >= WIDTH) & (lane < 2 * WIDTH)
    state = jnp.zeros((WIDTH, BLOCK), jnp.float32)
    for n in range(blocks):
        high = state.astype(jnp.bfloat16).astype(jnp.float32)
        starts[pl.ds(n * WIDTH, WIDTH), :] = jnp.where(takes_low, state - high, high).astype(
            jnp.bfloat16
        )
        state = decay * state + ends[pl.ds(n * WIDTH, WIDTH), :]

    for chunk in range(blocks // CHUNK):
        span = pl.ds(chunk * CHUNK * WIDTH, CHUNK * WIDTH)
        carried = jnp.dot(starts[span, :], lift_w[...], preferred_element_type=jnp.float32)
        gated = first[span, :] * (direct[span, :] + carried)
        sized = gated * gain_rows
        gained[pl.program_id(0), span, :] = sized
        squared = (gated * gated).reshape(CHUNK, 2, 8, BLOCK)
        squared = squared[:, 0] + squared[:, 1]
        size = jnp.abs(sized).reshape(CHUNK, 2, 8, BLOCK)
        size = jnp.maximum(size[:, 0], size[:, 1])
        rows = pl.ds(chunk * CHUNK, CHUNK)

        @pl.when(pl.program_id(0) == 0)
        def _():
            squares[rows] = squared
            peaks[rows] = size

        @pl.when(pl.program_id(0) != 0)
        def _():
            squares[rows] = squares[rows] + squared
            peaks[rows] = jnp.maximum(peaks[rows], size)

    @pl.when(pl.program_id(0) == pl.num_programs(0) - 1)
    def _():
        peak = jnp.maximum(jnp.max(peaks[...], axis=1), TINY)
        exponent = jnp.ceil(jnp.log2(peak))
        inverse = jnp.exp2(-exponent)
        total = (jnp.sum(squares[...], axis=1) * inverse) * inverse
        high = total.astype(jnp.bfloat16).astype(jnp.float32)
        rows_in[0] = exponent
        rows_in[1] = high
        rows_in[2] = total - high
        rows_in[3] = inverse
        local = gained.shape[0] * WIDTH
        for n in range(blocks):
            times = jnp.broadcast_to(rows_in[3, pl.ds(n, 1), :], (WIDTH, BLOCK))
            for g in range(gained.shape[0]):
                part = gained[g, pl.ds(n * WIDTH, WIDTH), :] * times
                row = (n % 2) * local + g * WIDTH
                coded_out[n // 2, row : row + WIDTH, :] = part * jnp.abs(part) * TOP
        for d in range(blocks // 2):
            pair = pl.ds(2 * d, 2)
            coded_out[d, 2 * local :, :] = jnp.concatenate(
                [
                    rows_in[0, pair, :], rows_in[1, pair, :], rows_in[2, pair, :],
                    jnp.zeros((2, BLOCK), jnp.float32),
                ],
                axis=0,
            )


def mix(place, streams, short_taps, rates, residues, skip, gain):
    channels, length = streams.shape[1:]
    blocks = length // BLOCK
    groups = channels // WIDTH
    rows = blocks * WIDTH
    short_taps = short_taps.transpose(0, 2, 1)
    rates = rates.T
    residues = residues.T
    skip = skip.reshape(-1, BLOCK)
    gain = gain.reshape(-1, BLOCK)
    whole = lambda array: pl.BlockSpec(array.shape, lambda g, place: (0,) * array.ndim)
    shape = (blocks // 2, 2 * channels + 8, BLOCK)
    return pl.pallas_call(
        mix_kernel,
        name="mix",
        grid_spec=pltpu.PrefetchScalarGridSpec(
            num_scalar_prefetch=1,
            grid=(groups,),
            in_specs=[
                pl.BlockSpec((3, WIDTH, length), lambda g, place: (0, g, 0)),
                whole(short_taps),
                whole(rates),
                whole(residues),
                whole(skip),
                whole(gain),
            ],
            out_specs=pl.BlockSpec(shape, lambda g, place: (0, 0, 0)),
            scratch_shapes=[
                pltpu.VMEM((3, 2 * BLOCK, 2 * BLOCK), jnp.bfloat16),
                pltpu.VMEM((2 * BLOCK, 4 * BLOCK), jnp.bfloat16),
                pltpu.VMEM((BLOCK, BLOCK), jnp.bfloat16),
                pltpu.VMEM((rows, BLOCK), jnp.float32),
                pltpu.VMEM((rows, BLOCK), jnp.float32),
                pltpu.VMEM((rows, BLOCK), jnp.float32),
                pltpu.VMEM((rows, BLOCK), jnp.bfloat16),
                pltpu.VMEM((blocks, 8, BLOCK), jnp.float32),
                pltpu.VMEM((blocks, 8, BLOCK), jnp.float32),
                pltpu.VMEM((groups, rows, BLOCK), jnp.float32),
                pltpu.VMEM((4, blocks, BLOCK), jnp.float32),
            ],
        ),
        out_shape=jax.ShapeDtypeStruct(shape, jnp.float32),
        compiler_params=pltpu.CompilerParams(dimension_semantics=("arbitrary",)),
    )(place, streams, short_taps, rates, residues, skip, gain)


def finish_kernel(coded, inverse_root, out):
    local = out.shape[0] // coded.shape[0]
    for k in range(coded.shape[0]):
        times = jnp.exp2(coded[k, 2 * local : 2 * local + 2, :]) * inverse_root[...]
        for h in range(2):
            value = coded[k, h * local : (h + 1) * local, :]
            size = jnp.sqrt(jnp.abs(value)) * jnp.broadcast_to(times[h : h + 1], value.shape)
            out[k * local : (k + 1) * local, h * BLOCK : (h + 1) * BLOCK] = jnp.where(
                value < 0, -size, size
            ).astype(jnp.bfloat16)


def finish(coded, inverse_root, channels):
    owners, rows = coded.shape[:2]
    return pl.pallas_call(
        finish_kernel,
        name="finish",
        grid=(owners // AT_ONCE,),
        in_specs=[
            pl.BlockSpec((AT_ONCE, rows, BLOCK), lambda i: (i, 0, 0)),
            pl.BlockSpec((2, BLOCK), lambda i: (0, 0)),
        ],
        out_specs=pl.BlockSpec((AT_ONCE * channels, 2 * BLOCK), lambda i: (i, 0)),
        out_shape=jax.ShapeDtypeStruct((owners * channels, 2 * BLOCK), jnp.bfloat16),
        compiler_params=pltpu.CompilerParams(dimension_semantics=("arbitrary",)),
    )(coded, inverse_root)


def summed_over(array, axis):
    count = lax.axis_size(axis)
    total = array
    for by in range(1, count):
        pairs = [(i, (i + by) % count) for i in range(count)]
        total = total + lax.ppermute(array, axis, pairs)
    return total


def shards(streams, short_taps, pole_rates, residues, skip, gain):
    channels = streams.shape[1]
    place = lax.axis_index(CTX)
    coded = mix(place.reshape(1), streams, short_taps, pole_rates, residues, skip, gain)
    moved = lax.all_to_all(coded.astype(jnp.float16), CTX, 0, 0, tiled=True)
    side = moved[:, 2 * channels :].astype(jnp.float32)
    size = jnp.exp2(side[:, 0:2])
    own = jnp.sum(((side[:, 2:4] + side[:, 4:6]) * size) * size, axis=0)
    mean_square = summed_over(own, "ch") / D
    inverse_root = TOP**-0.5 * lax.rsqrt(mean_square + 1e-05)
    return finish(moved.astype(jnp.float32), inverse_root, channels)


def solution(mesh):
    torus = Mesh(mesh.devices.reshape(8, 4, 2, mesh.shape["ch"]), ("ctx_0", "ctx_1", "ctx_2", "ch"))
    in_specs = (
        P(None, CH_CTX, None),
        P(None, "ch", None),
        P("ch", None),
        P("ch", None),
        P("ch"),
        P("ch"),
    )
    out_specs = P("ch", CTX)
    return jax.shard_map(
        shards, mesh=torus, in_specs=in_specs, out_specs=out_specs, check_vma=False
    )
```

```python
import jax
import jax.numpy as jnp
from jax import lax
from jax.experimental import pallas as pl
from jax.experimental.pallas import tpu as pltpu
from jax.sharding import Mesh
from jax.sharding import PartitionSpec as P

D = 8192
SHORT = 7
BLOCK = 128
WIDTH = 16
CTX = ("ctx_0", "ctx_1", "ctx_2")
CH_CTX = ("ch", "ctx_0", "ctx_1", "ctx_2")
CHUNK = 32
TOP = 32768.0
TINY = 1e-37
AT_ONCE = 16


def split(value):
    high = value.astype(jnp.bfloat16)
    low = (value - high.astype(jnp.float32)).astype(jnp.bfloat16)
    return high, low


def picked_column(array, first, step):
    rows = lax.broadcasted_iota(jnp.int32, (array.shape[0], BLOCK), 0)
    cols = lax.broadcasted_iota(jnp.int32, (array.shape[0], BLOCK), 1)
    return jnp.sum(jnp.where(cols == first + step * rows, array, 0.0), axis=1, keepdims=True)


def row_of(column, lanes):
    rows = lax.broadcasted_iota(jnp.int32, (column.shape[0], lanes), 0)
    cols = lax.broadcasted_iota(jnp.int32, (column.shape[0], lanes), 1)
    return jnp.sum(jnp.where(rows == cols, column, 0.0), axis=0, keepdims=True)


def channel_column(ref, group):
    per_row = BLOCK // WIDTH
    row = jnp.broadcast_to(ref[pl.ds(group // per_row, 1), :], (WIDTH, BLOCK))
    return picked_column(row, (group % per_row) * WIDTH, 1)


def toeplitz(row, rows):
    spread = jnp.broadcast_to(row, (rows, row.shape[1]))
    return pltpu.roll(spread, 0, 1, stride=1, stride_axis=0)


def mix_kernel(
    place, far, short_taps, rates, residues, skip, gain, gained_out, side_out,
    taps_w, conv_w, lift_w, first, direct, ends, starts, squares, peaks, streams, arrived,
):
    blocks = streams.shape[2] // BLOCK
    turn = pl.program_id(0)

    def fetch(g, chunk):
        lanes = pl.ds(chunk * CHUNK * BLOCK, CHUNK * BLOCK)
        at = (slice(None), pl.ds(pl.multiple_of(g * WIDTH, WIDTH), WIDTH), lanes)
        return pltpu.make_async_copy(far.at[at], streams.at[at], arrived.at[g, chunk])

    @pl.when(turn == 0)
    def _():
        for g in range(streams.shape[1] // WIDTH):
            for chunk in range(blocks // CHUNK):
                fetch(g, chunk).start()

    channel_rows = pl.ds(pl.multiple_of(turn * WIDTH, WIDTH), WIDTH)
    group = place[0] * pl.num_programs(0) + pl.program_id(0)
    rate = picked_column(rates[...], group, 0)
    residue = picked_column(residues[...], group, 0)
    skip_column = channel_column(skip, group)
    gain_column = channel_column(gain, group)
    zero = jnp.zeros((BLOCK, BLOCK), jnp.bfloat16)

    for m in range(3):
        row = row_of(picked_column(short_taps[m], group, 0), 2 * BLOCK)
        high, low = split(toeplitz(row, 2 * BLOCK)[:, BLOCK:])
        taps_w[m] = jnp.concatenate([high, low], axis=1)

    steps = lax.broadcasted_iota(jnp.int32, (WIDTH, BLOCK), 1).astype(jnp.float32)
    kernel_row = jnp.sum(residue * jnp.exp(-rate * steps), axis=0, keepdims=True)
    lags = toeplitz(kernel_row, BLOCK)
    at_row = lax.broadcasted_iota(jnp.int32, (BLOCK, BLOCK), 0)
    at_col = lax.broadcasted_iota(jnp.int32, (BLOCK, BLOCK), 1)
    high, low = split(jnp.where(at_col >= at_row, lags, 0.0))
    conv_w[:, : 2 * BLOCK] = jnp.concatenate(
        [jnp.concatenate([high, low], axis=1), jnp.concatenate([high, zero], axis=1)], axis=0
    )
    backward = jnp.exp(-rate * (BLOCK - 1 - steps))
    thrice = jnp.concatenate(
        [backward, backward, backward, jnp.zeros((BLOCK - 3 * WIDTH, BLOCK), jnp.float32)], axis=0
    ).T
    high, low = split(thrice)
    conv_w[:, 2 * BLOCK :] = jnp.concatenate(
        [jnp.concatenate([high, low], axis=1), jnp.concatenate([high, zero], axis=1)], axis=0
    )
    high, low = split(residue * jnp.exp(-rate * (steps + 1.0)))
    lift_w[...] = jnp.concatenate(
        [high, high, low, jnp.zeros((BLOCK - 3 * WIDTH, BLOCK), jnp.bfloat16)], axis=0
    )

    skip_rows = jnp.broadcast_to(
        skip_column[None], (CHUNK, WIDTH, BLOCK)
    ).reshape(CHUNK * WIDTH, BLOCK)
    gain_rows = jnp.broadcast_to(
        gain_column[None], (CHUNK, WIDTH, BLOCK)
    ).reshape(CHUNK * WIDTH, BLOCK)
    for chunk in range(blocks // CHUNK):
        span = pl.ds(chunk * CHUNK * WIDTH, CHUNK * WIDTH)
        fetch(turn, chunk).wait()
        filtered = []
        for m in range(3):
            pieces = []
            for n in range(chunk * CHUNK, (chunk + 1) * CHUNK):
                if n == 0:
                    here = streams[m, channel_rows, :BLOCK]
                    pieces.append(jnp.concatenate([jnp.zeros_like(here), here], axis=1))
                else:
                    pieces.append(streams[m, channel_rows, (n - 1) * BLOCK : (n + 1) * BLOCK])
            both = jnp.dot(
                jnp.concatenate(pieces, axis=0), taps_w[m], preferred_element_type=jnp.float32
            )
            filtered.append(both[:, :BLOCK] + both[:, BLOCK:])
        product = filtered[1] * filtered[2]
        high, low = split(product)
        terms = jnp.dot(
            jnp.concatenate([high, low], axis=1), conv_w[...], preferred_element_type=jnp.float32
        )
        first[span, :] = filtered[0]
        direct[span, :] = (terms[:, :BLOCK] + terms[:, BLOCK : 2 * BLOCK]) + skip_rows * product
        ends[span, :] = terms[:, 2 * BLOCK : 3 * BLOCK] + terms[:, 3 * BLOCK :]

    decay_column = jnp.exp(-rate * float(BLOCK))
    decay = jnp.broadcast_to(
        row_of(jnp.concatenate([decay_column] * 3, axis=0), BLOCK), (WIDTH, BLOCK)
    )
    lane = lax.broadcasted_iota(jnp.int32, (WIDTH, BLOCK), 1)
    takes_low = (lane >= WIDTH) & (lane < 2 * WIDTH)
    state = jnp.zeros((WIDTH, BLOCK), jnp.float32)
    for n in range(blocks):
        high = state.astype(jnp.bfloat16).astype(jnp.float32)
        starts[pl.ds(n * WIDTH, WIDTH), :] = jnp.where(takes_low, state - high, high).astype(
            jnp.bfloat16
        )
        state = decay * state + ends[pl.ds(n * WIDTH, WIDTH), :]

    for chunk in range(blocks // CHUNK):
        span = pl.ds(chunk * CHUNK * WIDTH, CHUNK * WIDTH)
        carried = jnp.dot(starts[span, :], lift_w[...], preferred_element_type=jnp.float32)
        gated = first[span, :] * (direct[span, :] + carried)
        sized = gated * gain_rows
        for k in range(CHUNK):
            n = chunk * CHUNK + k
            gained_out[n // 2, n % 2] = sized[k * WIDTH : (k + 1) * WIDTH]
        squared = (gated * gated).reshape(CHUNK, 2, 8, BLOCK)
        squared = squared[:, 0] + squared[:, 1]
        size = jnp.abs(sized).reshape(CHUNK, 2, 8, BLOCK)
        size = jnp.maximum(size[:, 0], size[:, 1])
        rows = pl.ds(chunk * CHUNK, CHUNK)

        @pl.when(pl.program_id(0) == 0)
        def _():
            squares[rows] = squared
            peaks[rows] = size

        @pl.when(pl.program_id(0) != 0)
        def _():
            squares[rows] = squares[rows] + squared
            peaks[rows] = jnp.maximum(peaks[rows], size)

    @pl.when(pl.program_id(0) == pl.num_programs(0) - 1)
    def _():
        peak = jnp.maximum(jnp.max(peaks[...], axis=1), TINY)
        exponent = jnp.ceil(jnp.log2(peak))
        inverse = jnp.exp2(-exponent)
        side_out[0] = jnp.sum(squares[...], axis=1)
        side_out[1] = exponent
        side_out[2] = inverse


def mix(place, streams, short_taps, rates, residues, skip, gain):
    channels, length = streams.shape[1:]
    blocks = length // BLOCK
    groups = channels // WIDTH
    rows = blocks * WIDTH
    short_taps = short_taps.transpose(0, 2, 1)
    rates = rates.T
    residues = residues.T
    skip = skip.reshape(-1, BLOCK)
    gain = gain.reshape(-1, BLOCK)
    whole = lambda array: pl.BlockSpec(array.shape, lambda g, place: (0,) * array.ndim)
    return pl.pallas_call(
        mix_kernel,
        name="mix",
        grid_spec=pltpu.PrefetchScalarGridSpec(
            num_scalar_prefetch=1,
            grid=(groups,),
            in_specs=[
                pl.BlockSpec(memory_space=pltpu.HBM),
                whole(short_taps),
                whole(rates),
                whole(residues),
                whole(skip),
                whole(gain),
            ],
            out_specs=[
                pl.BlockSpec((blocks // 2, 2, WIDTH, BLOCK), lambda g, place: (0, 0, g, 0)),
                pl.BlockSpec((3, blocks, BLOCK), lambda g, place: (0, 0, 0)),
            ],
            scratch_shapes=[
                pltpu.VMEM((3, 2 * BLOCK, 2 * BLOCK), jnp.bfloat16),
                pltpu.VMEM((2 * BLOCK, 4 * BLOCK), jnp.bfloat16),
                pltpu.VMEM((BLOCK, BLOCK), jnp.bfloat16),
                pltpu.VMEM((rows, BLOCK), jnp.float32),
                pltpu.VMEM((rows, BLOCK), jnp.float32),
                pltpu.VMEM((rows, BLOCK), jnp.float32),
                pltpu.VMEM((rows, BLOCK), jnp.bfloat16),
                pltpu.VMEM((blocks, 8, BLOCK), jnp.float32),
                pltpu.VMEM((blocks, 8, BLOCK), jnp.float32),
                pltpu.VMEM(streams.shape, jnp.bfloat16),
                pltpu.SemaphoreType.DMA((groups, blocks // CHUNK)),
            ],
        ),
        out_shape=[
            jax.ShapeDtypeStruct((blocks // 2, 2, channels, BLOCK), jnp.float32),
            jax.ShapeDtypeStruct((3, blocks, BLOCK), jnp.float32),
        ],
        compiler_params=pltpu.CompilerParams(
            dimension_semantics=("arbitrary",), vmem_limit_bytes=28 * 1024 * 1024
        ),
    )(place, pltpu.with_memory_space_constraint(streams, pltpu.HBM), short_taps, rates, residues, skip, gain)


def tail_kernel(own, *refs):
    *others, out = refs
    total = own[0]
    for other in others:
        total = total + other[...]
    total = jnp.maximum(total, TINY)
    exponent = jnp.ceil(jnp.log2(total))
    total = total * jnp.exp2(-exponent)
    high = total.astype(jnp.bfloat16).astype(jnp.float32)
    owners = out.shape[0]
    for at, value in enumerate((own[1], exponent, high, total - high)):
        value = value.reshape(owners, 2, BLOCK)
        out[:, 2 * at : 2 * at + 2, :] = value


def tail(side, others):
    blocks = side.shape[1]
    return pl.pallas_call(
        tail_kernel,
        name="tail",
        out_shape=jax.ShapeDtypeStruct((blocks // 2, 8, BLOCK), jnp.float32),
        compiler_params=pltpu.CompilerParams(vmem_limit_bytes=4 * 1024 * 1024),
    )(side, *others)


def finish_kernel(tails, coded, out, inverse_root):
    local = coded.shape[1] // 2
    step = pl.program_id(0)

    @pl.when(step == 0)
    def _():
        summed = (tails[:, 4:6, :] + tails[:, 6:8, :]) * jnp.exp2(tails[:, 2:4, :])
        inverse_root[...] = TOP**-0.5 * lax.rsqrt(jnp.sum(summed, axis=0) / D + 1e-05)

    for k in range(coded.shape[0]):
        times = jnp.exp2(tails[step * coded.shape[0] + k, 0:2, :]) * inverse_root[...]
        for h in range(2):
            value = coded[k, h * local : (h + 1) * local, :]
            root = value * lax.rsqrt(jnp.maximum(jnp.abs(value), 1e-20))
            out[k * local : (k + 1) * local, h * BLOCK : (h + 1) * BLOCK] = (
                root * jnp.broadcast_to(times[h : h + 1], value.shape)
            ).astype(jnp.bfloat16)


def finish(coded, channels):
    owners, rows = coded.shape[:2]
    return pl.pallas_call(
        finish_kernel,
        name="finish",
        grid=(owners // AT_ONCE,),
        in_specs=[
            pl.BlockSpec((owners, 8, BLOCK), lambda i: (0, rows // 8 - 1, 0)),
            pl.BlockSpec((AT_ONCE, 2 * channels, BLOCK), lambda i: (i, 0, 0)),
        ],
        out_specs=pl.BlockSpec((AT_ONCE * channels, 2 * BLOCK), lambda i: (i, 0)),
        out_shape=jax.ShapeDtypeStruct((owners * channels, 2 * BLOCK), jnp.bfloat16),
        scratch_shapes=[pltpu.VMEM((2, BLOCK), jnp.float32)],
        compiler_params=pltpu.CompilerParams(
            dimension_semantics=("arbitrary",), vmem_limit_bytes=12 * 1024 * 1024
        ),
    )(coded, coded)


def from_others(array, axis):
    count = lax.axis_size(axis)
    turns = [[(i, (i + by) % count) for i in range(count)] for by in range(1, count)]
    return [lax.ppermute(array, axis, pairs) for pairs in turns]


def shards(streams, short_taps, pole_rates, residues, skip, gain):
    channels = streams.shape[1]
    place = lax.axis_index(CTX)
    gained, side = mix(place.reshape(1), streams, short_taps, pole_rates, residues, skip, gain)
    owners = gained.shape[0]
    others = from_others(side[0], "ch")
    part = gained * side[2].reshape(owners, 2, 1, BLOCK)
    coded = (part * jnp.abs(part) * TOP).astype(jnp.float16)
    coded = jnp.pad(coded.reshape(owners, 2 * channels, BLOCK), ((0, 0), (0, 8), (0, 0)))
    coded = lax.optimization_barrier(coded)
    coded = lax.dynamic_update_slice(
        coded, tail(side, others).astype(jnp.float16), (0, 2 * channels, 0)
    )
    moved = lax.all_to_all(coded, CTX, 0, 0, tiled=True)
    return finish(moved.astype(jnp.float32), channels)


def solution(mesh):
    torus = Mesh(mesh.devices.reshape(8, 4, 2, mesh.shape["ch"]), ("ctx_0", "ctx_1", "ctx_2", "ch"))
    in_specs = (
        P(None, CH_CTX, None),
        P(None, "ch", None),
        P("ch", None),
        P("ch", None),
        P("ch"),
        P("ch"),
    )
    out_specs = P("ch", CTX)
    return jax.shard_map(
        shards, mesh=torus, in_specs=in_specs, out_specs=out_specs, check_vma=False
    )
```

```python
import jax
import jax.numpy as jnp
from jax import lax
from jax.experimental import pallas as pl
from jax.experimental.pallas import tpu as pltpu
from jax.sharding import Mesh
from jax.sharding import PartitionSpec as P

D = 8192
SHORT = 7
BLOCK = 128
WIDTH = 16
CTX = ("ctx_0", "ctx_1", "ctx_2")
CH_CTX = ("ch", "ctx_0", "ctx_1", "ctx_2")
CHUNK = 128
UNDER = 4
TOP = 32768.0
TINY = 1e-37
AT_ONCE = 16


def split(value):
    high = value.astype(jnp.bfloat16)
    low = (value - high.astype(jnp.float32)).astype(jnp.bfloat16)
    return high, low


def picked_column(array, first, step):
    rows = lax.broadcasted_iota(jnp.int32, (array.shape[0], BLOCK), 0)
    cols = lax.broadcasted_iota(jnp.int32, (array.shape[0], BLOCK), 1)
    return jnp.sum(jnp.where(cols == first + step * rows, array, 0.0), axis=1, keepdims=True)


def row_of(column, lanes):
    rows = lax.broadcasted_iota(jnp.int32, (column.shape[0], lanes), 0)
    cols = lax.broadcasted_iota(jnp.int32, (column.shape[0], lanes), 1)
    return jnp.sum(jnp.where(rows == cols, column, 0.0), axis=0, keepdims=True)


def channel_column(ref, group):
    per_row = BLOCK // WIDTH
    row = jnp.broadcast_to(ref[pl.ds(group // per_row, 1), :], (WIDTH, BLOCK))
    return picked_column(row, (group % per_row) * WIDTH, 1)


def toeplitz(row, rows):
    spread = jnp.broadcast_to(row, (rows, row.shape[1]))
    return pltpu.roll(spread, 0, 1, stride=1, stride_axis=0)


def mix_kernel(
    place, far, short_taps, rates, residues, skip, gain, gained_out, side_out,
    taps_w, conv_w, lift_w, first, direct, ends, starts, squares, peaks, streams, arrived,
):
    blocks = streams.shape[2] // BLOCK
    turn = pl.program_id(0)

    def fetch(g, chunk):
        lanes = pl.ds(chunk * CHUNK * BLOCK, CHUNK * BLOCK)
        at = (slice(None), pl.ds(pl.multiple_of(g * WIDTH, WIDTH), WIDTH), lanes)
        return pltpu.make_async_copy(far.at[at], streams.at[at], arrived.at[g, chunk])

    @pl.when(turn == 0)
    def _():
        for g in range(streams.shape[1] // WIDTH):
            for chunk in range(blocks // CHUNK):
                fetch(g, chunk).start()

    channel_rows = pl.ds(pl.multiple_of(turn * WIDTH, WIDTH), WIDTH)
    group = place[0] * pl.num_programs(0) + pl.program_id(0)
    rate = picked_column(rates[...], group, 0)
    residue = picked_column(residues[...], group, 0)
    skip_column = channel_column(skip, group)
    gain_column = channel_column(gain, group)
    zero = jnp.zeros((BLOCK, BLOCK), jnp.bfloat16)

    for m in range(3):
        row = row_of(picked_column(short_taps[m], group, 0), 2 * BLOCK)
        high, low = split(toeplitz(row, 2 * BLOCK)[:, BLOCK:])
        taps_w[m] = jnp.concatenate([high, low], axis=1)

    steps = lax.broadcasted_iota(jnp.int32, (WIDTH, BLOCK), 1).astype(jnp.float32)
    kernel_row = jnp.sum(residue * jnp.exp(-rate * steps), axis=0, keepdims=True)
    lags = toeplitz(kernel_row, BLOCK)
    at_row = lax.broadcasted_iota(jnp.int32, (BLOCK, BLOCK), 0)
    at_col = lax.broadcasted_iota(jnp.int32, (BLOCK, BLOCK), 1)
    high, low = split(jnp.where(at_col >= at_row, lags, 0.0))
    conv_w[:, : 2 * BLOCK] = jnp.concatenate(
        [jnp.concatenate([high, low], axis=1), jnp.concatenate([high, zero], axis=1)], axis=0
    )
    backward = jnp.exp(-rate * (BLOCK - 1 - steps))
    thrice = jnp.concatenate(
        [backward, backward, backward, jnp.zeros((BLOCK - 3 * WIDTH, BLOCK), jnp.float32)], axis=0
    ).T
    high, low = split(thrice)
    conv_w[:, 2 * BLOCK :] = jnp.concatenate(
        [jnp.concatenate([high, low], axis=1), jnp.concatenate([high, zero], axis=1)], axis=0
    )
    high, low = split(residue * jnp.exp(-rate * (steps + 1.0)))
    lift_w[...] = jnp.concatenate(
        [high, high, low, jnp.zeros((BLOCK - 3 * WIDTH, BLOCK), jnp.bfloat16)], axis=0
    )

    skip_rows = jnp.broadcast_to(
        skip_column[None], (CHUNK, WIDTH, BLOCK)
    ).reshape(CHUNK * WIDTH, BLOCK)
    gain_rows = jnp.broadcast_to(
        gain_column[None], (CHUNK, WIDTH, BLOCK)
    ).reshape(CHUNK * WIDTH, BLOCK)
    for chunk in range(blocks // CHUNK):
        span = pl.ds(chunk * CHUNK * WIDTH, CHUNK * WIDTH)
        fetch(turn, chunk).wait()
        filtered = []
        for m in range(3):
            pieces = []
            for n in range(chunk * CHUNK, (chunk + 1) * CHUNK):
                if n == 0:
                    here = streams[m, channel_rows, :BLOCK]
                    pieces.append(jnp.concatenate([jnp.zeros_like(here), here], axis=1))
                else:
                    pieces.append(streams[m, channel_rows, (n - 1) * BLOCK : (n + 1) * BLOCK])
            both = jnp.dot(
                jnp.concatenate(pieces, axis=0), taps_w[m], preferred_element_type=jnp.float32
            )
            filtered.append(both[:, :BLOCK] + both[:, BLOCK:])
        product = filtered[1] * filtered[2]
        high, low = split(product)
        terms = jnp.dot(
            jnp.concatenate([high, low], axis=1), conv_w[...], preferred_element_type=jnp.float32
        )
        first[span, :] = filtered[0]
        direct[span, :] = (terms[:, :BLOCK] + terms[:, BLOCK : 2 * BLOCK]) + skip_rows * product
        ends[span, :] = terms[:, 2 * BLOCK : 3 * BLOCK] + terms[:, 3 * BLOCK :]

    decay_column = jnp.exp(-rate * float(BLOCK))
    decay = jnp.broadcast_to(
        row_of(jnp.concatenate([decay_column] * 3, axis=0), BLOCK), (WIDTH, BLOCK)
    )
    lane = lax.broadcasted_iota(jnp.int32, (WIDTH, BLOCK), 1)
    takes_low = (lane >= WIDTH) & (lane < 2 * WIDTH)
    state = jnp.zeros((WIDTH, BLOCK), jnp.float32)
    powers = [decay]
    for k in range(1, UNDER):
        powers.append(powers[-1] * decay)
    for n in range(0, blocks, UNDER):
        at = [pl.ds((n + k) * WIDTH, WIDTH) for k in range(UNDER)]
        sums = [ends[at[0], :]]
        for k in range(1, UNDER):
            sums.append(decay * sums[-1] + ends[at[k], :])
        states = [state] + [powers[k] * state + sums[k] for k in range(UNDER)]
        for k in range(UNDER):
            high = states[k].astype(jnp.bfloat16).astype(jnp.float32)
            starts[at[k], :] = jnp.where(takes_low, states[k] - high, high).astype(jnp.bfloat16)
        state = states[UNDER]

    for chunk in range(blocks // CHUNK):
        span = pl.ds(chunk * CHUNK * WIDTH, CHUNK * WIDTH)
        carried = jnp.dot(starts[span, :], lift_w[...], preferred_element_type=jnp.float32)
        gated = first[span, :] * (direct[span, :] + carried)
        sized = gated * gain_rows
        for k in range(CHUNK):
            n = chunk * CHUNK + k
            gained_out[n // 2, n % 2] = sized[k * WIDTH : (k + 1) * WIDTH]
        squared = (gated * gated).reshape(CHUNK, 2, 8, BLOCK)
        squared = (squared[:, 0] + squared[:, 1]).reshape(CHUNK * 8, BLOCK)
        size = jnp.abs(sized).reshape(CHUNK, 2, 8, BLOCK)
        size = jnp.maximum(size[:, 0], size[:, 1]).reshape(CHUNK * 8, BLOCK)
        rows = pl.ds(chunk * CHUNK * 8, CHUNK * 8)

        @pl.when(pl.program_id(0) == 0)
        def _():
            squares[rows, :] = squared
            peaks[rows, :] = size

        @pl.when(pl.program_id(0) != 0)
        def _():
            squares[rows, :] = squares[rows, :] + squared
            peaks[rows, :] = jnp.maximum(peaks[rows, :], size)

    @pl.when(pl.program_id(0) == pl.num_programs(0) - 1)
    def _():
        total = squares[pl.ds(0, blocks, stride=8), :]
        peak = jnp.maximum(peaks[pl.ds(0, blocks, stride=8), :], TINY)
        for row in range(1, 8):
            total = total + squares[pl.ds(row, blocks, stride=8), :]
            peak = jnp.maximum(peak, peaks[pl.ds(row, blocks, stride=8), :])
        exponent = jnp.ceil(jnp.log2(peak))
        inverse = jnp.exp2(-exponent)
        side_out[0] = total
        side_out[1] = exponent
        side_out[2] = inverse


def mix(place, streams, short_taps, rates, residues, skip, gain):
    channels, length = streams.shape[1:]
    blocks = length // BLOCK
    groups = channels // WIDTH
    rows = blocks * WIDTH
    short_taps = short_taps.transpose(0, 2, 1)
    rates = rates.T
    residues = residues.T
    skip = skip.reshape(-1, BLOCK)
    gain = gain.reshape(-1, BLOCK)
    whole = lambda array: pl.BlockSpec(array.shape, lambda g, place: (0,) * array.ndim)
    return pl.pallas_call(
        mix_kernel,
        name="mix",
        grid_spec=pltpu.PrefetchScalarGridSpec(
            num_scalar_prefetch=1,
            grid=(groups,),
            in_specs=[
                pl.BlockSpec(memory_space=pltpu.HBM),
                whole(short_taps),
                whole(rates),
                whole(residues),
                whole(skip),
                whole(gain),
            ],
            out_specs=[
                pl.BlockSpec((blocks // 2, 2, WIDTH, BLOCK), lambda g, place: (0, 0, g, 0)),
                pl.BlockSpec((3, blocks, BLOCK), lambda g, place: (0, 0, 0)),
            ],
            scratch_shapes=[
                pltpu.VMEM((3, 2 * BLOCK, 2 * BLOCK), jnp.bfloat16),
                pltpu.VMEM((2 * BLOCK, 4 * BLOCK), jnp.bfloat16),
                pltpu.VMEM((BLOCK, BLOCK), jnp.bfloat16),
                pltpu.VMEM((rows, BLOCK), jnp.float32),
                pltpu.VMEM((rows, BLOCK), jnp.float32),
                pltpu.VMEM((rows, BLOCK), jnp.float32),
                pltpu.VMEM((rows, BLOCK), jnp.bfloat16),
                pltpu.VMEM((blocks * 8, BLOCK), jnp.float32),
                pltpu.VMEM((blocks * 8, BLOCK), jnp.float32),
                pltpu.VMEM(streams.shape, jnp.bfloat16),
                pltpu.SemaphoreType.DMA((groups, blocks // CHUNK)),
            ],
        ),
        out_shape=[
            jax.ShapeDtypeStruct((blocks // 2, 2, channels, BLOCK), jnp.float32),
            jax.ShapeDtypeStruct((3, blocks, BLOCK), jnp.float32),
        ],
        compiler_params=pltpu.CompilerParams(
            dimension_semantics=("arbitrary",), vmem_limit_bytes=28 * 1024 * 1024
        ),
    )(
        place,
        *(
            pltpu.with_memory_space_constraint(array, pltpu.HBM)
            for array in (streams, short_taps, rates, residues, skip, gain)
        ),
    )


def tail_kernel(own, *refs):
    *others, out = refs
    total = own[0]
    for other in others:
        total = total + other[...]
    total = jnp.maximum(total, TINY)
    exponent = jnp.ceil(jnp.log2(total))
    total = total * jnp.exp2(-exponent)
    high = total.astype(jnp.bfloat16).astype(jnp.float32)
    owners = out.shape[0]
    for at, value in enumerate((own[1], exponent, high, total - high)):
        value = value.reshape(owners, 2, BLOCK)
        out[:, 2 * at : 2 * at + 2, :] = value


def tail(side, others):
    blocks = side.shape[1]
    return pl.pallas_call(
        tail_kernel,
        name="tail",
        out_shape=jax.ShapeDtypeStruct((blocks // 2, 8, BLOCK), jnp.float32),
        compiler_params=pltpu.CompilerParams(vmem_limit_bytes=4 * 1024 * 1024),
    )(side, *others)


def finish_kernel(tails, coded, out, inverse_root):
    local = coded.shape[1] // 2
    step = pl.program_id(0)

    @pl.when(step == 0)
    def _():
        summed = (tails[:, 4:6, :] + tails[:, 6:8, :]) * jnp.exp2(tails[:, 2:4, :])
        inverse_root[...] = TOP**-0.5 * lax.rsqrt(jnp.sum(summed, axis=0) / D + 1e-05)

    for k in range(coded.shape[0]):
        times = jnp.exp2(tails[step * coded.shape[0] + k, 0:2, :]) * inverse_root[...]
        for h in range(2):
            value = coded[k, h * local : (h + 1) * local, :]
            root = value * lax.rsqrt(jnp.maximum(jnp.abs(value), 1e-20))
            out[k * local : (k + 1) * local, h * BLOCK : (h + 1) * BLOCK] = (
                root * jnp.broadcast_to(times[h : h + 1], value.shape)
            ).astype(jnp.bfloat16)


def finish(coded, channels):
    owners, rows = coded.shape[:2]
    return pl.pallas_call(
        finish_kernel,
        name="finish",
        grid=(owners // AT_ONCE,),
        in_specs=[
            pl.BlockSpec((owners, 8, BLOCK), lambda i: (0, rows // 8 - 1, 0)),
            pl.BlockSpec((AT_ONCE, 2 * channels, BLOCK), lambda i: (i, 0, 0)),
        ],
        out_specs=pl.BlockSpec((AT_ONCE * channels, 2 * BLOCK), lambda i: (i, 0)),
        out_shape=jax.ShapeDtypeStruct((owners * channels, 2 * BLOCK), jnp.bfloat16),
        scratch_shapes=[pltpu.VMEM((2, BLOCK), jnp.float32)],
        compiler_params=pltpu.CompilerParams(
            dimension_semantics=("arbitrary",), vmem_limit_bytes=12 * 1024 * 1024
        ),
    )(coded, coded)


def from_others(array, axis):
    count = lax.axis_size(axis)
    turns = [[(i, (i + by) % count) for i in range(count)] for by in range(1, count)]
    return [lax.ppermute(array, axis, pairs) for pairs in turns]


def shards(streams, short_taps, pole_rates, residues, skip, gain):
    channels = streams.shape[1]
    place = lax.axis_index(CTX)
    gained, side = mix(place.reshape(1), streams, short_taps, pole_rates, residues, skip, gain)
    owners = gained.shape[0]
    others = from_others(side[0], "ch")
    part = gained * side[2].reshape(owners, 2, 1, BLOCK)
    coded = (part * jnp.abs(part) * TOP).astype(jnp.float16)
    coded = jnp.pad(coded.reshape(owners, 2 * channels, BLOCK), ((0, 0), (0, 8), (0, 0)))
    coded = lax.optimization_barrier(coded)
    coded = lax.dynamic_update_slice(
        coded, tail(side, others).astype(jnp.float16), (0, 2 * channels, 0)
    )
    moved = lax.all_to_all(coded, CTX, 0, 0, tiled=True)
    return finish(moved.astype(jnp.float32), channels)


def solution(mesh):
    torus = Mesh(mesh.devices.reshape(8, 4, 2, mesh.shape["ch"]), ("ctx_0", "ctx_1", "ctx_2", "ch"))
    in_specs = (
        P(None, CH_CTX, None),
        P(None, "ch", None),
        P("ch", None),
        P("ch", None),
        P("ch"),
        P("ch"),
    )
    out_specs = P("ch", CTX)
    return jax.shard_map(
        shards, mesh=torus, in_specs=in_specs, out_specs=out_specs, check_vma=False
    )
```

```python
import jax
import jax.numpy as jnp
from jax import lax
from jax.experimental import pallas as pl
from jax.experimental.pallas import tpu as pltpu
from jax.sharding import Mesh
from jax.sharding import PartitionSpec as P

D = 8192
BLOCK = 128
WIDTH = 16
CTX = ("ctx_0", "ctx_1", "ctx_2")
CH_CTX = ("ch", "ctx_0", "ctx_1", "ctx_2")
CHUNK = 128
UNDER = 4
TOP = 32768.0
TINY = 1e-37
AT_ONCE = 16


def split(value):
    high = value.astype(jnp.bfloat16)
    low = (value - high.astype(jnp.float32)).astype(jnp.bfloat16)
    return high, low


def picked_column(array, first, step):
    rows = lax.broadcasted_iota(jnp.int32, (array.shape[0], BLOCK), 0)
    cols = lax.broadcasted_iota(jnp.int32, (array.shape[0], BLOCK), 1)
    return jnp.sum(jnp.where(cols == first + step * rows, array, 0.0), axis=1, keepdims=True)


def row_of(column, lanes):
    rows = lax.broadcasted_iota(jnp.int32, (column.shape[0], lanes), 0)
    cols = lax.broadcasted_iota(jnp.int32, (column.shape[0], lanes), 1)
    return jnp.sum(jnp.where(rows == cols, column, 0.0), axis=0, keepdims=True)


def channel_column(ref, group):
    per_row = BLOCK // WIDTH
    row = jnp.broadcast_to(ref[pl.ds(group // per_row, 1), :], (WIDTH, BLOCK))
    return picked_column(row, (group % per_row) * WIDTH, 1)


def toeplitz(row, rows):
    spread = jnp.broadcast_to(row, (rows, row.shape[1]))
    return pltpu.roll(spread, 0, 1, stride=1, stride_axis=0)


def mix_kernel(
    place, far, short_taps, rates, residues, skip, gain, gained_out, side_out, tail_out,
    taps_w, conv_w, lift_w, first, direct, ends, starts, squares, peaks, streams, arrived,
):
    blocks = streams.shape[2] // BLOCK
    turn = pl.program_id(0)

    def fetch(g, chunk):
        lanes = pl.ds(chunk * CHUNK * BLOCK, CHUNK * BLOCK)
        at = (slice(None), pl.ds(pl.multiple_of(g * WIDTH, WIDTH), WIDTH), lanes)
        return pltpu.make_async_copy(far.at[at], streams.at[at], arrived.at[g, chunk])

    @pl.when(turn == 0)
    def _():
        for g in range(streams.shape[1] // WIDTH):
            for chunk in range(blocks // CHUNK):
                fetch(g, chunk).start()

    channel_rows = pl.ds(pl.multiple_of(turn * WIDTH, WIDTH), WIDTH)
    group = place[0] * pl.num_programs(0) + pl.program_id(0)
    rate = picked_column(rates[...], group, 0)
    residue = picked_column(residues[...], group, 0)
    skip_column = channel_column(skip, group)
    gain_column = channel_column(gain, group)
    zero = jnp.zeros((BLOCK, BLOCK), jnp.bfloat16)

    for m in range(3):
        row = row_of(picked_column(short_taps[m], group, 0), 2 * BLOCK)
        high, low = split(toeplitz(row, 2 * BLOCK)[:, BLOCK:])
        taps_w[m] = jnp.concatenate([high, low], axis=1)

    steps = lax.broadcasted_iota(jnp.int32, (WIDTH, BLOCK), 1).astype(jnp.float32)
    kernel_row = jnp.sum(residue * jnp.exp(-rate * steps), axis=0, keepdims=True)
    lags = toeplitz(kernel_row, BLOCK)
    at_row = lax.broadcasted_iota(jnp.int32, (BLOCK, BLOCK), 0)
    at_col = lax.broadcasted_iota(jnp.int32, (BLOCK, BLOCK), 1)
    high, low = split(jnp.where(at_col >= at_row, lags, 0.0))
    conv_w[:, : 2 * BLOCK] = jnp.concatenate(
        [jnp.concatenate([high, low], axis=1), jnp.concatenate([high, zero], axis=1)], axis=0
    )
    backward = jnp.exp(-rate * (BLOCK - 1 - steps))
    thrice = jnp.concatenate(
        [backward, backward, backward, jnp.zeros((BLOCK - 3 * WIDTH, BLOCK), jnp.float32)], axis=0
    ).T
    high, low = split(thrice)
    conv_w[:, 2 * BLOCK :] = jnp.concatenate(
        [jnp.concatenate([high, low], axis=1), jnp.concatenate([high, zero], axis=1)], axis=0
    )
    high, low = split(residue * jnp.exp(-rate * (steps + 1.0)))
    lift_w[...] = jnp.concatenate(
        [high, high, low, jnp.zeros((BLOCK - 3 * WIDTH, BLOCK), jnp.bfloat16)], axis=0
    )

    skip_rows = jnp.broadcast_to(
        skip_column[None], (CHUNK, WIDTH, BLOCK)
    ).reshape(CHUNK * WIDTH, BLOCK)
    gain_rows = jnp.broadcast_to(
        gain_column[None], (CHUNK, WIDTH, BLOCK)
    ).reshape(CHUNK * WIDTH, BLOCK)
    for chunk in range(blocks // CHUNK):
        span = pl.ds(chunk * CHUNK * WIDTH, CHUNK * WIDTH)
        fetch(turn, chunk).wait()
        filtered = []
        for m in range(3):
            pieces = []
            for n in range(chunk * CHUNK, (chunk + 1) * CHUNK):
                if n == 0:
                    here = streams[m, channel_rows, :BLOCK]
                    pieces.append(jnp.concatenate([jnp.zeros_like(here), here], axis=1))
                else:
                    pieces.append(streams[m, channel_rows, (n - 1) * BLOCK : (n + 1) * BLOCK])
            both = jnp.dot(
                jnp.concatenate(pieces, axis=0), taps_w[m], preferred_element_type=jnp.float32
            )
            filtered.append(both[:, :BLOCK] + both[:, BLOCK:])
        product = filtered[1] * filtered[2]
        high, low = split(product)
        terms = jnp.dot(
            jnp.concatenate([high, low], axis=1), conv_w[...], preferred_element_type=jnp.float32
        )
        first[span, :] = filtered[0]
        direct[span, :] = (terms[:, :BLOCK] + terms[:, BLOCK : 2 * BLOCK]) + skip_rows * product
        ends[span, :] = terms[:, 2 * BLOCK : 3 * BLOCK] + terms[:, 3 * BLOCK :]

    decay_column = jnp.exp(-rate * float(BLOCK))
    decay = jnp.broadcast_to(
        row_of(jnp.concatenate([decay_column] * 3, axis=0), BLOCK), (WIDTH, BLOCK)
    )
    lane = lax.broadcasted_iota(jnp.int32, (WIDTH, BLOCK), 1)
    takes_low = (lane >= WIDTH) & (lane < 2 * WIDTH)
    state = jnp.zeros((WIDTH, BLOCK), jnp.float32)
    powers = [decay]
    for _ in range(1, UNDER):
        powers.append(powers[-1] * decay)
    for n in range(0, blocks, UNDER):
        at = [pl.ds((n + k) * WIDTH, WIDTH) for k in range(UNDER)]
        sums = [ends[at[0], :]]
        for k in range(1, UNDER):
            sums.append(decay * sums[-1] + ends[at[k], :])
        states = [state] + [powers[k] * state + sums[k] for k in range(UNDER)]
        for k in range(UNDER):
            high = states[k].astype(jnp.bfloat16).astype(jnp.float32)
            starts[at[k], :] = jnp.where(takes_low, states[k] - high, high).astype(jnp.bfloat16)
        state = states[UNDER]

    for chunk in range(blocks // CHUNK):
        span = pl.ds(chunk * CHUNK * WIDTH, CHUNK * WIDTH)
        carried = jnp.dot(starts[span, :], lift_w[...], preferred_element_type=jnp.float32)
        gated = first[span, :] * (direct[span, :] + carried)
        sized = gated * gain_rows
        for k in range(CHUNK):
            n = chunk * CHUNK + k
            gained_out[n // 2, n % 2] = sized[k * WIDTH : (k + 1) * WIDTH]
        squared = (gated * gated).reshape(CHUNK, 2, 8, BLOCK)
        squared = (squared[:, 0] + squared[:, 1]).reshape(CHUNK * 8, BLOCK)
        size = jnp.abs(sized).reshape(CHUNK, 2, 8, BLOCK)
        size = jnp.maximum(size[:, 0], size[:, 1]).reshape(CHUNK * 8, BLOCK)
        rows = pl.ds(chunk * CHUNK * 8, CHUNK * 8)

        @pl.when(pl.program_id(0) == 0)
        def _():
            squares[rows, :] = squared
            peaks[rows, :] = size

        @pl.when(pl.program_id(0) != 0)
        def _():
            squares[rows, :] = squares[rows, :] + squared
            peaks[rows, :] = jnp.maximum(peaks[rows, :], size)

    @pl.when(pl.program_id(0) == pl.num_programs(0) - 1)
    def _():
        total = squares[pl.ds(0, blocks, stride=8), :]
        peak = jnp.maximum(peaks[pl.ds(0, blocks, stride=8), :], TINY)
        for row in range(1, 8):
            total = total + squares[pl.ds(row, blocks, stride=8), :]
            peak = jnp.maximum(peak, peaks[pl.ds(row, blocks, stride=8), :])
        exponent = jnp.ceil(jnp.log2(peak))
        inverse = jnp.exp2(-exponent)
        side_out[0] = total
        side_out[1] = inverse
        tail_out[:, 0:2, :] = exponent.reshape(blocks // 2, 2, BLOCK)
        tail_out[:, 2:8, :] = jnp.zeros((blocks // 2, 6, BLOCK), jnp.float32)


def mix(place, streams, short_taps, rates, residues, skip, gain):
    channels, length = streams.shape[1:]
    blocks = length // BLOCK
    groups = channels // WIDTH
    rows = blocks * WIDTH
    short_taps = short_taps.transpose(0, 2, 1)
    rates = rates.T
    residues = residues.T
    skip = skip.reshape(-1, BLOCK)
    gain = gain.reshape(-1, BLOCK)
    whole = lambda array: pl.BlockSpec(array.shape, lambda g, place: (0,) * array.ndim)
    return pl.pallas_call(
        mix_kernel,
        name="mix",
        grid_spec=pltpu.PrefetchScalarGridSpec(
            num_scalar_prefetch=1,
            grid=(groups,),
            in_specs=[
                pl.BlockSpec(memory_space=pltpu.HBM),
                whole(short_taps),
                whole(rates),
                whole(residues),
                whole(skip),
                whole(gain),
            ],
            out_specs=[
                pl.BlockSpec((blocks // 2, 2, WIDTH, BLOCK), lambda g, place: (0, 0, g, 0)),
                pl.BlockSpec((2, blocks, BLOCK), lambda g, place: (0, 0, 0)),
                pl.BlockSpec((blocks // 2, 8, BLOCK), lambda g, place: (0, 0, 0)),
            ],
            scratch_shapes=[
                pltpu.VMEM((3, 2 * BLOCK, 2 * BLOCK), jnp.bfloat16),
                pltpu.VMEM((2 * BLOCK, 4 * BLOCK), jnp.bfloat16),
                pltpu.VMEM((BLOCK, BLOCK), jnp.bfloat16),
                pltpu.VMEM((rows, BLOCK), jnp.float32),
                pltpu.VMEM((rows, BLOCK), jnp.float32),
                pltpu.VMEM((rows, BLOCK), jnp.float32),
                pltpu.VMEM((rows, BLOCK), jnp.bfloat16),
                pltpu.VMEM((blocks * 8, BLOCK), jnp.float32),
                pltpu.VMEM((blocks * 8, BLOCK), jnp.float32),
                pltpu.VMEM(streams.shape, jnp.bfloat16),
                pltpu.SemaphoreType.DMA((groups, blocks // CHUNK)),
            ],
        ),
        out_shape=[
            jax.ShapeDtypeStruct((blocks // 2, 2, channels, BLOCK), jnp.float32),
            jax.ShapeDtypeStruct((2, blocks, BLOCK), jnp.float32),
            jax.ShapeDtypeStruct((blocks // 2, 8, BLOCK), jnp.float32),
        ],
        compiler_params=pltpu.CompilerParams(
            dimension_semantics=("arbitrary",), vmem_limit_bytes=28 * 1024 * 1024
        ),
    )(
        place,
        *(
            pltpu.with_memory_space_constraint(array, pltpu.HBM)
            for array in (streams, short_taps, rates, residues, skip, gain)
        ),
    )


def finish_kernel(coded, mean_square, out):
    local = (coded.shape[1] - 8) // 2
    inverse_root = TOP**-0.5 * lax.rsqrt(mean_square[...] + 1e-05)
    for k in range(coded.shape[0]):
        times = jnp.exp2(coded[k, 2 * local : 2 * local + 2, :]) * inverse_root
        for h in range(2):
            value = coded[k, h * local : (h + 1) * local, :]
            root = value * lax.rsqrt(jnp.maximum(jnp.abs(value), 1e-20))
            out[k * local : (k + 1) * local, h * BLOCK : (h + 1) * BLOCK] = (
                root * jnp.broadcast_to(times[h : h + 1], value.shape)
            ).astype(jnp.bfloat16)


def finish(coded, mean_square, channels):
    owners, rows = coded.shape[:2]
    return pl.pallas_call(
        finish_kernel,
        name="finish",
        grid=(owners // AT_ONCE,),
        in_specs=[
            pl.BlockSpec((AT_ONCE, rows, BLOCK), lambda i: (i, 0, 0)),
            pl.BlockSpec((2, BLOCK), lambda i: (0, 0)),
        ],
        out_specs=pl.BlockSpec((AT_ONCE * channels, 2 * BLOCK), lambda i: (i, 0)),
        out_shape=jax.ShapeDtypeStruct((owners * channels, 2 * BLOCK), jnp.bfloat16),
        compiler_params=pltpu.CompilerParams(
            dimension_semantics=("arbitrary",), vmem_limit_bytes=12 * 1024 * 1024
        ),
    )(coded, mean_square)


def with_partner(array, axis, bit):
    pairs = [(i, i ^ bit) for i in range(lax.axis_size(axis))]
    return lax.ppermute(array, axis, pairs)


def half_summed(halves, axis, bit):
    mine = (lax.axis_index(axis) // bit) % 2 == 0
    kept = jnp.where(mine, halves[0], halves[1])
    given = jnp.where(mine, halves[1], halves[0])
    return kept + with_partner(given, axis, bit)


def summed_for_owner(squares):
    z, x, core = (lax.axis_size(axis) for axis in CTX)
    bit = lax.axis_size("ch") // 2
    while bit:
        squares = squares + with_partner(squares, "ch", bit)
        bit //= 2
    squares = squares.reshape(z, x, core, 2, BLOCK).transpose(2, 1, 0, 3, 4)
    for axis, count in ((CTX[2], core), (CTX[1], x), (CTX[0], z)):
        bit = count // 2
        while bit:
            squares = squares.reshape(2, squares.shape[0] // 2, *squares.shape[1:])
            squares = half_summed(squares, axis, bit)
            bit //= 2
        squares = squares.reshape(squares.shape[1:])
    return squares


def shards(streams, short_taps, pole_rates, residues, skip, gain):
    channels = streams.shape[1]
    place = lax.axis_index(CTX)
    gained, side, tails = mix(
        place.reshape(1), streams, short_taps, pole_rates, residues, skip, gain
    )
    owners = gained.shape[0]
    part = gained * side[1].reshape(owners, 2, 1, BLOCK)
    coded = (part * jnp.abs(part) * TOP).astype(jnp.float16)
    coded = jnp.pad(coded.reshape(owners, 2 * channels, BLOCK), ((0, 0), (0, 8), (0, 0)))
    coded = lax.optimization_barrier(coded)
    coded = lax.dynamic_update_slice(
        coded, tails.astype(jnp.float16), (0, 2 * channels, 0)
    )
    moved = lax.all_to_all(coded, CTX, 0, 0, tiled=True)
    mean_square = summed_for_owner(side[0]) / D
    return finish(moved.astype(jnp.float32), mean_square, channels)


def solution(mesh):
    torus = Mesh(mesh.devices.reshape(8, 4, 2, mesh.shape["ch"]), ("ctx_0", "ctx_1", "ctx_2", "ch"))
    in_specs = (
        P(None, CH_CTX, None),
        P(None, "ch", None),
        P("ch", None),
        P("ch", None),
        P("ch"),
        P("ch"),
    )
    out_specs = P("ch", CTX)
    return jax.shard_map(
        shards, mesh=torus, in_specs=in_specs, out_specs=out_specs, check_vma=False
    )
```

```python
import jax
import jax.numpy as jnp
from jax import lax
from jax.experimental import pallas as pl
from jax.experimental.pallas import tpu as pltpu
from jax.sharding import Mesh
from jax.sharding import PartitionSpec as P

D = 8192
BLOCK = 128
WIDTH = 16
CTX = ("ctx_0", "ctx_1", "ctx_2")
CH_CTX = ("ch", "ctx_0", "ctx_1", "ctx_2")
CHUNK = 128
UNDER = 4
TOP = 32768.0
TINY = 1e-37
AT_ONCE = 16


def split(value):
    high = value.astype(jnp.bfloat16)
    low = (value - high.astype(jnp.float32)).astype(jnp.bfloat16)
    return high, low


def picked_column(array, first, step):
    rows = lax.broadcasted_iota(jnp.int32, (array.shape[0], BLOCK), 0)
    cols = lax.broadcasted_iota(jnp.int32, (array.shape[0], BLOCK), 1)
    return jnp.sum(jnp.where(cols == first + step * rows, array, 0.0), axis=1, keepdims=True)


def row_of(column, lanes):
    rows = lax.broadcasted_iota(jnp.int32, (column.shape[0], lanes), 0)
    cols = lax.broadcasted_iota(jnp.int32, (column.shape[0], lanes), 1)
    return jnp.sum(jnp.where(rows == cols, column, 0.0), axis=0, keepdims=True)


def channel_column(ref, group):
    per_row = BLOCK // WIDTH
    row = jnp.broadcast_to(ref[pl.ds(group // per_row, 1), :], (WIDTH, BLOCK))
    return picked_column(row, (group % per_row) * WIDTH, 1)


def toeplitz(row, rows):
    spread = jnp.broadcast_to(row, (rows, row.shape[1]))
    return pltpu.roll(spread, 0, 1, stride=1, stride_axis=0)


def mix_kernel(
    place, far, short_taps, rates, residues, skip, gain, coded_out, square_out,
    taps_w, conv_w, lift_w, first, direct, ends, starts, squares, peaks, streams, arrived,
    gained, inverses,
):
    blocks = streams.shape[2] // BLOCK
    turn = pl.program_id(0)

    def fetch(g, chunk):
        lanes = pl.ds(chunk * CHUNK * BLOCK, CHUNK * BLOCK)
        at = (slice(None), pl.ds(pl.multiple_of(g * WIDTH, WIDTH), WIDTH), lanes)
        return pltpu.make_async_copy(far.at[at], streams.at[at], arrived.at[g, chunk])

    @pl.when(turn == 0)
    def _():
        for g in range(streams.shape[1] // WIDTH):
            for chunk in range(blocks // CHUNK):
                fetch(g, chunk).start()

    channel_rows = pl.ds(pl.multiple_of(turn * WIDTH, WIDTH), WIDTH)
    group = place[0] * pl.num_programs(0) + pl.program_id(0)
    rate = picked_column(rates[...], group, 0)
    residue = picked_column(residues[...], group, 0)
    skip_column = channel_column(skip, group)
    gain_column = channel_column(gain, group)
    zero = jnp.zeros((BLOCK, BLOCK), jnp.bfloat16)

    for m in range(3):
        row = row_of(picked_column(short_taps[m], group, 0), 2 * BLOCK)
        high, low = split(toeplitz(row, 2 * BLOCK)[:, BLOCK:])
        taps_w[m] = jnp.concatenate([high, low], axis=1)

    steps = lax.broadcasted_iota(jnp.int32, (WIDTH, BLOCK), 1).astype(jnp.float32)
    kernel_row = jnp.sum(residue * jnp.exp(-rate * steps), axis=0, keepdims=True)
    lags = toeplitz(kernel_row, BLOCK)
    at_row = lax.broadcasted_iota(jnp.int32, (BLOCK, BLOCK), 0)
    at_col = lax.broadcasted_iota(jnp.int32, (BLOCK, BLOCK), 1)
    high, low = split(jnp.where(at_col >= at_row, lags, 0.0))
    conv_w[:, : 2 * BLOCK] = jnp.concatenate(
        [jnp.concatenate([high, low], axis=1), jnp.concatenate([high, zero], axis=1)], axis=0
    )
    backward = jnp.exp(-rate * (BLOCK - 1 - steps))
    thrice = jnp.concatenate(
        [backward, backward, backward, jnp.zeros((BLOCK - 3 * WIDTH, BLOCK), jnp.float32)], axis=0
    ).T
    high, low = split(thrice)
    conv_w[:, 2 * BLOCK :] = jnp.concatenate(
        [jnp.concatenate([high, low], axis=1), jnp.concatenate([high, zero], axis=1)], axis=0
    )
    high, low = split(residue * jnp.exp(-rate * (steps + 1.0)))
    lift_w[...] = jnp.concatenate(
        [high, high, low, jnp.zeros((BLOCK - 3 * WIDTH, BLOCK), jnp.bfloat16)], axis=0
    )

    skip_rows = jnp.broadcast_to(
        skip_column[None], (CHUNK, WIDTH, BLOCK)
    ).reshape(CHUNK * WIDTH, BLOCK)
    gain_rows = jnp.broadcast_to(
        gain_column[None], (CHUNK, WIDTH, BLOCK)
    ).reshape(CHUNK * WIDTH, BLOCK)
    for chunk in range(blocks // CHUNK):
        span = pl.ds(chunk * CHUNK * WIDTH, CHUNK * WIDTH)
        fetch(turn, chunk).wait()
        filtered = []
        for m in range(3):
            pieces = []
            for n in range(chunk * CHUNK, (chunk + 1) * CHUNK):
                if n == 0:
                    here = streams[m, channel_rows, :BLOCK]
                    pieces.append(jnp.concatenate([jnp.zeros_like(here), here], axis=1))
                else:
                    pieces.append(streams[m, channel_rows, (n - 1) * BLOCK : (n + 1) * BLOCK])
            both = jnp.dot(
                jnp.concatenate(pieces, axis=0), taps_w[m], preferred_element_type=jnp.float32
            )
            filtered.append(both[:, :BLOCK] + both[:, BLOCK:])
        product = filtered[1] * filtered[2]
        high, low = split(product)
        terms = jnp.dot(
            jnp.concatenate([high, low], axis=1), conv_w[...], preferred_element_type=jnp.float32
        )
        first[span, :] = filtered[0]
        direct[span, :] = (terms[:, :BLOCK] + terms[:, BLOCK : 2 * BLOCK]) + skip_rows * product
        ends[span, :] = terms[:, 2 * BLOCK : 3 * BLOCK] + terms[:, 3 * BLOCK :]

    decay_column = jnp.exp(-rate * float(BLOCK))
    decay = jnp.broadcast_to(
        row_of(jnp.concatenate([decay_column] * 3, axis=0), BLOCK), (WIDTH, BLOCK)
    )
    lane = lax.broadcasted_iota(jnp.int32, (WIDTH, BLOCK), 1)
    takes_low = (lane >= WIDTH) & (lane < 2 * WIDTH)
    state = jnp.zeros((WIDTH, BLOCK), jnp.float32)
    powers = [decay]
    for _ in range(1, UNDER):
        powers.append(powers[-1] * decay)
    for n in range(0, blocks, UNDER):
        at = [pl.ds((n + k) * WIDTH, WIDTH) for k in range(UNDER)]
        sums = [ends[at[0], :]]
        for k in range(1, UNDER):
            sums.append(decay * sums[-1] + ends[at[k], :])
        states = [state] + [powers[k] * state + sums[k] for k in range(UNDER)]
        for k in range(UNDER):
            high = states[k].astype(jnp.bfloat16).astype(jnp.float32)
            starts[at[k], :] = jnp.where(takes_low, states[k] - high, high).astype(jnp.bfloat16)
        state = states[UNDER]

    for chunk in range(blocks // CHUNK):
        span = pl.ds(chunk * CHUNK * WIDTH, CHUNK * WIDTH)
        carried = jnp.dot(starts[span, :], lift_w[...], preferred_element_type=jnp.float32)
        gated = first[span, :] * (direct[span, :] + carried)
        sized = gated * gain_rows
        gained[turn, span, :] = sized
        squared = (gated * gated).reshape(CHUNK, 2, 8, BLOCK)
        squared = (squared[:, 0] + squared[:, 1]).reshape(CHUNK * 8, BLOCK)
        size = jnp.abs(sized).reshape(CHUNK, 2, 8, BLOCK)
        size = jnp.maximum(size[:, 0], size[:, 1]).reshape(CHUNK * 8, BLOCK)
        rows = pl.ds(chunk * CHUNK * 8, CHUNK * 8)

        @pl.when(pl.program_id(0) == 0)
        def _():
            squares[rows, :] = squared
            peaks[rows, :] = size

        @pl.when(pl.program_id(0) != 0)
        def _():
            squares[rows, :] = squares[rows, :] + squared
            peaks[rows, :] = jnp.maximum(peaks[rows, :], size)

    @pl.when(pl.program_id(0) == pl.num_programs(0) - 1)
    def _():
        total = squares[pl.ds(0, blocks, stride=8), :]
        peak = jnp.maximum(peaks[pl.ds(0, blocks, stride=8), :], TINY)
        for row in range(1, 8):
            total = total + squares[pl.ds(row, blocks, stride=8), :]
            peak = jnp.maximum(peak, peaks[pl.ds(row, blocks, stride=8), :])
        exponent = jnp.ceil(jnp.log2(peak))
        inverse = jnp.exp2(-exponent)
        square_out[...] = total
        inverses[...] = inverse
        local = streams.shape[1]
        for n in range(blocks):
            times = jnp.broadcast_to(inverses[pl.ds(n, 1), :], (WIDTH, BLOCK))
            for g in range(local // WIDTH):
                part = gained[g, pl.ds(n * WIDTH, WIDTH), :] * times
                row = (n % 2) * local + g * WIDTH
                coded_out[n // 2, row : row + WIDTH, :] = part * jnp.abs(part) * TOP
        owners = blocks // 2
        coded_out[:, 2 * local : 2 * local + 2, :] = exponent.reshape(owners, 2, BLOCK)
        coded_out[:, 2 * local + 2 :, :] = jnp.zeros((owners, 6, BLOCK), jnp.float32)


def mix(place, streams, short_taps, rates, residues, skip, gain):
    channels, length = streams.shape[1:]
    blocks = length // BLOCK
    groups = channels // WIDTH
    rows = blocks * WIDTH
    short_taps = short_taps.transpose(0, 2, 1)
    rates = rates.T
    residues = residues.T
    skip = skip.reshape(-1, BLOCK)
    gain = gain.reshape(-1, BLOCK)
    shape = (blocks // 2, 2 * channels + 8, BLOCK)
    whole = lambda array: pl.BlockSpec(array.shape, lambda g, place: (0,) * array.ndim)
    return pl.pallas_call(
        mix_kernel,
        name="mix",
        grid_spec=pltpu.PrefetchScalarGridSpec(
            num_scalar_prefetch=1,
            grid=(groups,),
            in_specs=[
                pl.BlockSpec(memory_space=pltpu.HBM),
                whole(short_taps),
                whole(rates),
                whole(residues),
                whole(skip),
                whole(gain),
            ],
            out_specs=[
                pl.BlockSpec(shape, lambda g, place: (0, 0, 0)),
                pl.BlockSpec((blocks, BLOCK), lambda g, place: (0, 0)),
            ],
            scratch_shapes=[
                pltpu.VMEM((3, 2 * BLOCK, 2 * BLOCK), jnp.bfloat16),
                pltpu.VMEM((2 * BLOCK, 4 * BLOCK), jnp.bfloat16),
                pltpu.VMEM((BLOCK, BLOCK), jnp.bfloat16),
                pltpu.VMEM((rows, BLOCK), jnp.float32),
                pltpu.VMEM((rows, BLOCK), jnp.float32),
                pltpu.VMEM((rows, BLOCK), jnp.float32),
                pltpu.VMEM((rows, BLOCK), jnp.bfloat16),
                pltpu.VMEM((blocks * 8, BLOCK), jnp.float32),
                pltpu.VMEM((blocks * 8, BLOCK), jnp.float32),
                pltpu.VMEM(streams.shape, jnp.bfloat16),
                pltpu.SemaphoreType.DMA((groups, blocks // CHUNK)),
                pltpu.VMEM((groups, rows, BLOCK), jnp.float32),
                pltpu.VMEM((blocks, BLOCK), jnp.float32),
            ],
        ),
        out_shape=[
            jax.ShapeDtypeStruct(shape, jnp.float32),
            jax.ShapeDtypeStruct((blocks, BLOCK), jnp.float32),
        ],
        compiler_params=pltpu.CompilerParams(
            dimension_semantics=("arbitrary",), vmem_limit_bytes=28 * 1024 * 1024
        ),
    )(
        place,
        *(
            pltpu.with_memory_space_constraint(array, pltpu.HBM)
            for array in (streams, short_taps, rates, residues, skip, gain)
        ),
    )


def finish_kernel(coded, mean_square, out):
    local = (coded.shape[1] - 8) // 2
    inverse_root = TOP**-0.5 * lax.rsqrt(mean_square[...] + 1e-05)
    for k in range(coded.shape[0]):
        times = jnp.exp2(coded[k, 2 * local : 2 * local + 2, :]) * inverse_root
        for h in range(2):
            value = coded[k, h * local : (h + 1) * local, :]
            root = value * lax.rsqrt(jnp.maximum(jnp.abs(value), 1e-20))
            out[k * local : (k + 1) * local, h * BLOCK : (h + 1) * BLOCK] = (
                root * jnp.broadcast_to(times[h : h + 1], value.shape)
            ).astype(jnp.bfloat16)


def finish(coded, mean_square, channels):
    owners, rows = coded.shape[:2]
    return pl.pallas_call(
        finish_kernel,
        name="finish",
        grid=(owners // AT_ONCE,),
        in_specs=[
            pl.BlockSpec((AT_ONCE, rows, BLOCK), lambda i: (i, 0, 0)),
            pl.BlockSpec((2, BLOCK), lambda i: (0, 0)),
        ],
        out_specs=pl.BlockSpec((AT_ONCE * channels, 2 * BLOCK), lambda i: (i, 0)),
        out_shape=jax.ShapeDtypeStruct((owners * channels, 2 * BLOCK), jnp.bfloat16),
        compiler_params=pltpu.CompilerParams(
            dimension_semantics=("arbitrary",), vmem_limit_bytes=12 * 1024 * 1024
        ),
    )(coded, mean_square)


def scattered(pieces, axis):
    count = lax.axis_size(axis)
    twice = jnp.concatenate([pieces, pieces], axis=0)
    turned = lax.dynamic_slice_in_dim(twice, lax.axis_index(axis), count, 0)
    total = turned[0]
    for by in range(1, count):
        pairs = [(i, (i + by) % count) for i in range(count)]
        total = total + lax.ppermute(turned[by], axis, pairs)
    return total


def with_partner(array, axis, bit):
    pairs = [(i, i ^ bit) for i in range(lax.axis_size(axis))]
    return array + lax.ppermute(array, axis, pairs)


def summed_for_owner(squares):
    z, x, core = (lax.axis_size(axis) for axis in CTX)
    squares = squares.reshape(z, x, core, 2, BLOCK).transpose(2, 1, 0, 3, 4)
    for axis in reversed(CTX):
        squares = scattered(squares, axis)
    return squares


def shards(streams, short_taps, pole_rates, residues, skip, gain):
    channels = streams.shape[1]
    place = lax.axis_index(CTX)
    coded, squares = mix(
        place.reshape(1), streams, short_taps, pole_rates, residues, skip, gain
    )
    squares = with_partner(squares, "ch", 1)
    moved = lax.all_to_all(coded.astype(jnp.float16), CTX, 0, 0, tiled=True)
    mean_square = summed_for_owner(with_partner(squares, "ch", 2)) / D
    return finish(moved.astype(jnp.float32), mean_square, channels)


def solution(mesh):
    torus = Mesh(mesh.devices.reshape(8, 4, 2, mesh.shape["ch"]), ("ctx_0", "ctx_1", "ctx_2", "ch"))
    in_specs = (
        P(None, CH_CTX, None),
        P(None, "ch", None),
        P("ch", None),
        P("ch", None),
        P("ch"),
        P("ch"),
    )
    out_specs = P("ch", CTX)
    return jax.shard_map(
        shards, mesh=torus, in_specs=in_specs, out_specs=out_specs, check_vma=False
    )
```

```python
import jax
import jax.numpy as jnp
from jax import lax
from jax.experimental import pallas as pl
from jax.experimental.pallas import tpu as pltpu
from jax.sharding import Mesh
from jax.sharding import PartitionSpec as P

D = 8192
BLOCK = 128
WIDTH = 16
CTX = ("ctx_0", "ctx_1", "ctx_2")
CH_CTX = ("ch", "ctx_0", "ctx_1", "ctx_2")
UNDER = 4
TOP = 32768.0
TINY = 1e-37
AT_ONCE = 16


def split(value):
    high = value.astype(jnp.bfloat16)
    low = (value - high.astype(jnp.float32)).astype(jnp.bfloat16)
    return high, low


def picked_column(array, first, step):
    rows = lax.broadcasted_iota(jnp.int32, (array.shape[0], BLOCK), 0)
    cols = lax.broadcasted_iota(jnp.int32, (array.shape[0], BLOCK), 1)
    return jnp.sum(jnp.where(cols == first + step * rows, array, 0.0), axis=1, keepdims=True)


def row_of(column, lanes):
    rows = lax.broadcasted_iota(jnp.int32, (column.shape[0], lanes), 0)
    cols = lax.broadcasted_iota(jnp.int32, (column.shape[0], lanes), 1)
    return jnp.sum(jnp.where(rows == cols, column, 0.0), axis=0, keepdims=True)


def channel_column(ref, group):
    per_row = BLOCK // WIDTH
    row = jnp.broadcast_to(ref[pl.ds(group // per_row, 1), :], (WIDTH, BLOCK))
    return picked_column(row, (group % per_row) * WIDTH, 1)


def toeplitz(row, rows):
    spread = jnp.broadcast_to(row, (rows, row.shape[1]))
    return pltpu.roll(spread, 0, 1, stride=1, stride_axis=0)


def all_rows(column, blocks):
    width = column.shape[0]
    return jnp.broadcast_to(column[None], (blocks, width, BLOCK)).reshape(blocks * width, BLOCK)


def weights(group, short_taps, rates, residues, taps_w, conv_w, lift_w):
    rate = picked_column(rates[...], group, 0)
    residue = picked_column(residues[...], group, 0)
    zero = jnp.zeros((BLOCK, BLOCK), jnp.bfloat16)

    for m in range(3):
        row = row_of(picked_column(short_taps[m], group, 0), 2 * BLOCK)
        high, low = split(toeplitz(row, 2 * BLOCK)[:, BLOCK:])
        taps_w[m] = jnp.concatenate([high, low], axis=1)

    steps = lax.broadcasted_iota(jnp.int32, (WIDTH, BLOCK), 1).astype(jnp.float32)
    kernel_row = jnp.sum(residue * jnp.exp(-rate * steps), axis=0, keepdims=True)
    lags = toeplitz(kernel_row, BLOCK)
    at_row = lax.broadcasted_iota(jnp.int32, (BLOCK, BLOCK), 0)
    at_col = lax.broadcasted_iota(jnp.int32, (BLOCK, BLOCK), 1)
    high, low = split(jnp.where(at_col >= at_row, lags, 0.0))
    conv_w[:, : 2 * BLOCK] = jnp.concatenate(
        [jnp.concatenate([high, low], axis=1), jnp.concatenate([high, zero], axis=1)], axis=0
    )
    backward = jnp.exp(-rate * (BLOCK - 1 - steps))
    thrice = jnp.concatenate(
        [backward, backward, backward, jnp.zeros((BLOCK - 3 * WIDTH, BLOCK), jnp.float32)], axis=0
    ).T
    high, low = split(thrice)
    conv_w[:, 2 * BLOCK :] = jnp.concatenate(
        [jnp.concatenate([high, low], axis=1), jnp.concatenate([high, zero], axis=1)], axis=0
    )
    high, low = split(residue * jnp.exp(-rate * (steps + 1.0)))
    lift_w[...] = jnp.concatenate(
        [high, high, low, jnp.zeros((BLOCK - 3 * WIDTH, BLOCK), jnp.bfloat16)], axis=0
    )

    decay_column = jnp.exp(-rate * float(BLOCK))
    decay = jnp.broadcast_to(
        row_of(jnp.concatenate([decay_column] * 3, axis=0), BLOCK), (WIDTH, BLOCK)
    )
    return decay


def scan(decay, ends, starts):
    blocks = ends.shape[0] // WIDTH
    lane = lax.broadcasted_iota(jnp.int32, (WIDTH, BLOCK), 1)
    takes_low = (lane >= WIDTH) & (lane < 2 * WIDTH)
    state = jnp.zeros((WIDTH, BLOCK), jnp.float32)
    powers = [decay]
    for _ in range(1, UNDER):
        powers.append(powers[-1] * decay)
    for n in range(0, blocks, UNDER):
        at = [pl.ds((n + k) * WIDTH, WIDTH) for k in range(UNDER)]
        sums = [ends[at[0], :]]
        for k in range(1, UNDER):
            sums.append(decay * sums[-1] + ends[at[k], :])
        states = [state] + [powers[k] * state + sums[k] for k in range(UNDER)]
        for k in range(UNDER):
            high = states[k].astype(jnp.bfloat16).astype(jnp.float32)
            starts[at[k], :] = jnp.where(takes_low, states[k] - high, high).astype(jnp.bfloat16)
        state = states[UNDER]


def mix_kernel(
    place, far, far_taps, far_rates, far_residues, far_skip, far_gain, coded_out, square_out,
    short_taps, rates, residues, skip, gain, streams, arrived,
    taps_w, conv_w, lift_w, first, direct, ends, starts, squares, peaks, gained, inverses,
):
    blocks = streams.shape[2] // BLOCK
    local = streams.shape[1]
    groups = local // WIDTH
    everything = slice(None)
    smalls = [
        pltpu.make_async_copy(source, target, arrived.at[3 * groups + at])
        for at, (source, target) in enumerate(
            (
                (far_taps, short_taps), (far_rates, rates), (far_residues, residues),
                (far_skip, skip), (far_gain, gain),
            )
        )
    ]
    bulks = []
    for g in range(groups):
        for m in range(3):
            at = (m, pl.ds(g * WIDTH, WIDTH), everything)
            bulks.append(
                pltpu.make_async_copy(far.at[at], streams.at[at], arrived.at[3 * g + m])
            )
    for copy in smalls + bulks:
        copy.start()
    for copy in smalls:
        copy.wait()
    decays = []
    for g in range(groups):
        decays.append(
            weights(
                place[0] * groups + g, short_taps, rates, residues,
                taps_w.at[g], conv_w.at[g], lift_w.at[g],
            )
        )
    for g in range(groups):
        for copy in bulks[3 * g : 3 * g + 3]:
            copy.wait()
        filtered = []
        for m in range(3):
            pieces = []
            for n in range(blocks):
                rows = slice(g * WIDTH, (g + 1) * WIDTH)
                if n == 0:
                    here = streams[m, rows, :BLOCK]
                    pieces.append(jnp.concatenate([jnp.zeros_like(here), here], axis=1))
                else:
                    pieces.append(streams[m, rows, (n - 1) * BLOCK : (n + 1) * BLOCK])
            both = jnp.dot(
                jnp.concatenate(pieces, axis=0), taps_w[g, m], preferred_element_type=jnp.float32
            )
            filtered.append(both[:, :BLOCK] + both[:, BLOCK:])
        product = filtered[1] * filtered[2]
        high, low = split(product)
        terms = jnp.dot(
            jnp.concatenate([high, low], axis=1), conv_w[g], preferred_element_type=jnp.float32
        )
        skip_rows = all_rows(channel_column(skip, place[0] * groups + g), blocks)
        first[g] = filtered[0]
        direct[g] = (terms[:, :BLOCK] + terms[:, BLOCK : 2 * BLOCK]) + skip_rows * product
        ends[g] = terms[:, 2 * BLOCK : 3 * BLOCK] + terms[:, 3 * BLOCK :]
        scan(decays[g], ends.at[g], starts.at[g])
        carried = jnp.dot(starts[g], lift_w[g], preferred_element_type=jnp.float32)
        gated = first[g] * (direct[g] + carried)
        sized = gated * all_rows(channel_column(gain, place[0] * groups + g), blocks)
        gained[g] = sized
        squared = (gated * gated).reshape(blocks, 2, 8, BLOCK)
        squared = (squared[:, 0] + squared[:, 1]).reshape(blocks * 8, BLOCK)
        size = jnp.abs(sized).reshape(blocks, 2, 8, BLOCK)
        size = jnp.maximum(size[:, 0], size[:, 1]).reshape(blocks * 8, BLOCK)
        if g:
            squared = squares[...] + squared
            size = jnp.maximum(peaks[...], size)
        squares[...] = squared
        peaks[...] = size

    total = squares[pl.ds(0, blocks, stride=8), :]
    peak = jnp.maximum(peaks[pl.ds(0, blocks, stride=8), :], TINY)
    for row in range(1, 8):
        total = total + squares[pl.ds(row, blocks, stride=8), :]
        peak = jnp.maximum(peak, peaks[pl.ds(row, blocks, stride=8), :])
    exponent = jnp.ceil(jnp.log2(peak))
    inverses[...] = jnp.exp2(-exponent)
    square_out[...] = total
    for n in range(blocks):
        times = jnp.broadcast_to(inverses[pl.ds(n, 1), :], (WIDTH, BLOCK))
        for g in range(groups):
            part = gained[g, pl.ds(n * WIDTH, WIDTH), :] * times
            row = (n % 2) * local + g * WIDTH
            coded_out[n // 2, row : row + WIDTH, :] = part * jnp.abs(part) * TOP
    owners = blocks // 2
    coded_out[:, 2 * local : 2 * local + 2, :] = exponent.reshape(owners, 2, BLOCK)
    coded_out[:, 2 * local + 2 :, :] = jnp.zeros((owners, 6, BLOCK), jnp.float32)


def mix(place, streams, short_taps, rates, residues, skip, gain):
    channels, length = streams.shape[1:]
    blocks = length // BLOCK
    groups = channels // WIDTH
    rows = blocks * WIDTH
    short_taps = short_taps.transpose(0, 2, 1)
    rates = rates.T
    residues = residues.T
    skip = skip.reshape(-1, BLOCK)
    gain = gain.reshape(-1, BLOCK)
    shape = (blocks // 2, 2 * channels + 8, BLOCK)
    inputs = (streams, short_taps, rates, residues, skip, gain)
    return pl.pallas_call(
        mix_kernel,
        name="mix",
        grid_spec=pltpu.PrefetchScalarGridSpec(
            num_scalar_prefetch=1,
            grid=(1,),
            in_specs=[pl.BlockSpec(memory_space=pltpu.HBM)] * len(inputs),
            out_specs=[
                pl.BlockSpec(shape, lambda g, place: (0, 0, 0)),
                pl.BlockSpec((blocks, BLOCK), lambda g, place: (0, 0)),
            ],
            scratch_shapes=[
                *(pltpu.VMEM(array.shape, array.dtype) for array in inputs[1:]),
                pltpu.VMEM(streams.shape, jnp.bfloat16),
                pltpu.SemaphoreType.DMA((3 * groups + 5,)),
                pltpu.VMEM((groups, 3, 2 * BLOCK, 2 * BLOCK), jnp.bfloat16),
                pltpu.VMEM((groups, 2 * BLOCK, 4 * BLOCK), jnp.bfloat16),
                pltpu.VMEM((groups, BLOCK, BLOCK), jnp.bfloat16),
                pltpu.VMEM((groups, rows, BLOCK), jnp.float32),
                pltpu.VMEM((groups, rows, BLOCK), jnp.float32),
                pltpu.VMEM((groups, rows, BLOCK), jnp.float32),
                pltpu.VMEM((groups, rows, BLOCK), jnp.bfloat16),
                pltpu.VMEM((blocks * 8, BLOCK), jnp.float32),
                pltpu.VMEM((blocks * 8, BLOCK), jnp.float32),
                pltpu.VMEM((groups, rows, BLOCK), jnp.float32),
                pltpu.VMEM((blocks, BLOCK), jnp.float32),
            ],
        ),
        out_shape=[
            jax.ShapeDtypeStruct(shape, jnp.float32),
            jax.ShapeDtypeStruct((blocks, BLOCK), jnp.float32),
        ],
        compiler_params=pltpu.CompilerParams(
            dimension_semantics=("arbitrary",), vmem_limit_bytes=28 * 1024 * 1024
        ),
    )(
        place,
        *(
            pltpu.with_memory_space_constraint(array, pltpu.HBM)
            for array in inputs
        ),
    )


def finish_kernel(coded, mean_square, out):
    local = (coded.shape[1] - 8) // 2
    inverse_root = TOP**-0.5 * lax.rsqrt(mean_square[...] + 1e-05)
    for k in range(coded.shape[0]):
        times = jnp.exp2(coded[k, 2 * local : 2 * local + 2, :]) * inverse_root
        for h in range(2):
            value = coded[k, h * local : (h + 1) * local, :]
            root = value * lax.rsqrt(jnp.maximum(jnp.abs(value), 1e-20))
            out[k * local : (k + 1) * local, h * BLOCK : (h + 1) * BLOCK] = (
                root * jnp.broadcast_to(times[h : h + 1], value.shape)
            ).astype(jnp.bfloat16)


def finish(coded, mean_square, channels):
    owners, rows = coded.shape[:2]
    return pl.pallas_call(
        finish_kernel,
        name="finish",
        grid=(owners // AT_ONCE,),
        in_specs=[
            pl.BlockSpec((AT_ONCE, rows, BLOCK), lambda i: (i, 0, 0)),
            pl.BlockSpec((2, BLOCK), lambda i: (0, 0)),
        ],
        out_specs=pl.BlockSpec((AT_ONCE * channels, 2 * BLOCK), lambda i: (i, 0)),
        out_shape=jax.ShapeDtypeStruct((owners * channels, 2 * BLOCK), jnp.bfloat16),
        compiler_params=pltpu.CompilerParams(
            dimension_semantics=("arbitrary",), vmem_limit_bytes=12 * 1024 * 1024
        ),
    )(coded, mean_square)


def scattered(pieces, axis):
    count = lax.axis_size(axis)
    twice = jnp.concatenate([pieces, pieces], axis=0)
    turned = lax.dynamic_slice_in_dim(twice, lax.axis_index(axis), count, 0)
    total = turned[0]
    for by in range(1, count):
        pairs = [(i, (i + by) % count) for i in range(count)]
        total = total + lax.ppermute(turned[by], axis, pairs)
    return total


def with_partner(array, axis, bit):
    pairs = [(i, i ^ bit) for i in range(lax.axis_size(axis))]
    return array + lax.ppermute(array, axis, pairs)


def summed_for_owner(squares):
    z, x, core = (lax.axis_size(axis) for axis in CTX)
    squares = squares.reshape(z, x, core, 2, BLOCK).transpose(2, 1, 0, 3, 4)
    for axis in reversed(CTX):
        squares = scattered(squares, axis)
    return squares


def shards(streams, short_taps, pole_rates, residues, skip, gain):
    channels = streams.shape[1]
    place = lax.axis_index(CTX)
    coded, squares = mix(
        place.reshape(1), streams, short_taps, pole_rates, residues, skip, gain
    )
    squares = with_partner(squares, "ch", 1)
    moved = lax.all_to_all(coded.astype(jnp.float16), CTX, 0, 0, tiled=True)
    mean_square = summed_for_owner(with_partner(squares, "ch", 2)) / D
    return finish(moved.astype(jnp.float32), mean_square, channels)


def solution(mesh):
    torus = Mesh(mesh.devices.reshape(8, 4, 2, mesh.shape["ch"]), ("ctx_0", "ctx_1", "ctx_2", "ch"))
    in_specs = (
        P(None, CH_CTX, None),
        P(None, "ch", None),
        P("ch", None),
        P("ch", None),
        P("ch"),
        P("ch"),
    )
    out_specs = P("ch", CTX)
    return jax.shard_map(
        shards, mesh=torus, in_specs=in_specs, out_specs=out_specs, check_vma=False
    )
```

```python
import jax
import jax.numpy as jnp
from jax import lax
from jax.experimental import pallas as pl
from jax.experimental.pallas import tpu as pltpu
from jax.sharding import Mesh
from jax.sharding import PartitionSpec as P

D = 8192
BLOCK = 128
WIDTH = 16
CTX = ("ctx_0", "ctx_1", "ctx_2")
CH_CTX = ("ch", "ctx_0", "ctx_1", "ctx_2")
UNDER = 4
TOP = 32768.0
TINY = 1e-37
AT_ONCE = 16


def split(value):
    high = value.astype(jnp.bfloat16)
    low = (value - high.astype(jnp.float32)).astype(jnp.bfloat16)
    return high, low


def picked_column(array, first, step):
    rows = lax.broadcasted_iota(jnp.int32, (array.shape[0], BLOCK), 0)
    cols = lax.broadcasted_iota(jnp.int32, (array.shape[0], BLOCK), 1)
    return jnp.sum(jnp.where(cols == first + step * rows, array, 0.0), axis=1, keepdims=True)


def row_of(column, lanes):
    rows = lax.broadcasted_iota(jnp.int32, (column.shape[0], lanes), 0)
    cols = lax.broadcasted_iota(jnp.int32, (column.shape[0], lanes), 1)
    return jnp.sum(jnp.where(rows == cols, column, 0.0), axis=0, keepdims=True)


def channel_column(ref, group):
    per_row = BLOCK // WIDTH
    row = jnp.broadcast_to(ref[pl.ds(group // per_row, 1), :], (WIDTH, BLOCK))
    return picked_column(row, (group % per_row) * WIDTH, 1)


def toeplitz(row, rows):
    spread = jnp.broadcast_to(row, (rows, row.shape[1]))
    return pltpu.roll(spread, 0, 1, stride=1, stride_axis=0)


def all_rows(column, blocks):
    width = column.shape[0]
    return jnp.broadcast_to(column[None], (blocks, width, BLOCK)).reshape(blocks * width, BLOCK)


def weights(group, short_taps, rates, residues, taps_w, conv_w, lift_w):
    rate = picked_column(rates[...], group, 0)
    residue = picked_column(residues[...], group, 0)
    zero = jnp.zeros((BLOCK, BLOCK), jnp.bfloat16)

    for m in range(3):
        row = row_of(picked_column(short_taps[m], group, 0), 2 * BLOCK)
        high, low = split(toeplitz(row, 2 * BLOCK)[:, BLOCK:])
        taps_w[m] = jnp.concatenate([high, low], axis=1)

    steps = lax.broadcasted_iota(jnp.int32, (WIDTH, BLOCK), 1).astype(jnp.float32)
    kernel_row = jnp.sum(residue * jnp.exp(-rate * steps), axis=0, keepdims=True)
    lags = toeplitz(kernel_row, BLOCK)
    at_row = lax.broadcasted_iota(jnp.int32, (BLOCK, BLOCK), 0)
    at_col = lax.broadcasted_iota(jnp.int32, (BLOCK, BLOCK), 1)
    high, low = split(jnp.where(at_col >= at_row, lags, 0.0))
    conv_w[:, : 2 * BLOCK] = jnp.concatenate(
        [jnp.concatenate([high, low], axis=1), jnp.concatenate([high, zero], axis=1)], axis=0
    )
    backward = jnp.exp(-rate * (BLOCK - 1 - steps))
    thrice = jnp.concatenate(
        [backward, backward, backward, jnp.zeros((BLOCK - 3 * WIDTH, BLOCK), jnp.float32)], axis=0
    ).T
    high, low = split(thrice)
    conv_w[:, 2 * BLOCK :] = jnp.concatenate(
        [jnp.concatenate([high, low], axis=1), jnp.concatenate([high, zero], axis=1)], axis=0
    )
    high, low = split(residue * jnp.exp(-rate * (steps + 1.0)))
    lift_w[...] = jnp.concatenate(
        [high, high, low, jnp.zeros((BLOCK - 3 * WIDTH, BLOCK), jnp.bfloat16)], axis=0
    )

    decay_column = jnp.exp(-rate * float(BLOCK))
    decay = jnp.broadcast_to(
        row_of(jnp.concatenate([decay_column] * 3, axis=0), BLOCK), (WIDTH, BLOCK)
    )
    return decay


def scan(decay, ends, starts):
    blocks = ends.shape[0] // WIDTH
    lane = lax.broadcasted_iota(jnp.int32, (WIDTH, BLOCK), 1)
    takes_low = (lane >= WIDTH) & (lane < 2 * WIDTH)
    state = jnp.zeros((WIDTH, BLOCK), jnp.float32)
    powers = [decay]
    for _ in range(1, UNDER):
        powers.append(powers[-1] * decay)
    for n in range(0, blocks, UNDER):
        at = [pl.ds((n + k) * WIDTH, WIDTH) for k in range(UNDER)]
        sums = [ends[at[0], :]]
        for k in range(1, UNDER):
            sums.append(decay * sums[-1] + ends[at[k], :])
        states = [state] + [powers[k] * state + sums[k] for k in range(UNDER)]
        for k in range(UNDER):
            high = states[k].astype(jnp.bfloat16).astype(jnp.float32)
            starts[at[k], :] = jnp.where(takes_low, states[k] - high, high).astype(jnp.bfloat16)
        state = states[UNDER]


def mix_kernel(
    place, far, far_taps, far_rates, far_residues, far_skip, far_gain, coded_out, square_out,
    short_taps, rates, residues, skip, gain, streams, arrived,
    taps_w, conv_w, lift_w, first, direct, ends, starts, squares, peaks, gained, inverses,
):
    blocks = streams.shape[2] // BLOCK
    local = streams.shape[1]
    groups = local // WIDTH
    everything = slice(None)
    smalls = [
        pltpu.make_async_copy(source, target, arrived.at[3 * groups + at])
        for at, (source, target) in enumerate(
            (
                (far_taps, short_taps), (far_rates, rates), (far_residues, residues),
                (far_skip, skip), (far_gain, gain),
            )
        )
    ]
    bulks = []
    for g in range(groups):
        for m in range(3):
            at = (m, pl.ds(g * WIDTH, WIDTH), everything)
            bulks.append(
                pltpu.make_async_copy(far.at[at], streams.at[at], arrived.at[3 * g + m])
            )
    for copy in smalls + bulks:
        copy.start()
    for copy in smalls:
        copy.wait()
    decays = {}

    def prepare(g):
        decays[g] = weights(
            place[0] * groups + g, short_taps, rates, residues,
            taps_w.at[g], conv_w.at[g], lift_w.at[g],
        )

    def arrive(g):
        for copy in bulks[3 * g : 3 * g + 3]:
            copy.wait()

    def front(g):
        rows = slice(g * WIDTH, (g + 1) * WIDTH)
        filtered = []
        for m in range(3):
            here = streams[m, rows, :BLOCK]
            pieces = [jnp.concatenate([jnp.zeros_like(here), here], axis=1)]
            for n in range(1, blocks):
                pieces.append(streams[m, rows, (n - 1) * BLOCK : (n + 1) * BLOCK])
            both = jnp.dot(
                jnp.concatenate(pieces, axis=0), taps_w[g, m], preferred_element_type=jnp.float32
            )
            filtered.append(both[:, :BLOCK] + both[:, BLOCK:])
        product = filtered[1] * filtered[2]
        high, low = split(product)
        terms = jnp.dot(
            jnp.concatenate([high, low], axis=1), conv_w[g], preferred_element_type=jnp.float32
        )
        skip_rows = all_rows(channel_column(skip, place[0] * groups + g), blocks)
        first[g] = filtered[0]
        direct[g] = (terms[:, :BLOCK] + terms[:, BLOCK : 2 * BLOCK]) + skip_rows * product
        ends[g] = terms[:, 2 * BLOCK : 3 * BLOCK] + terms[:, 3 * BLOCK :]

    def back(g):
        scan(decays[g], ends.at[g], starts.at[g])
        carried = jnp.dot(starts[g], lift_w[g], preferred_element_type=jnp.float32)
        gated = first[g] * (direct[g] + carried)
        sized = gated * all_rows(channel_column(gain, place[0] * groups + g), blocks)
        gained[g] = sized
        squared = (gated * gated).reshape(blocks, 2, 8, BLOCK)
        squared = (squared[:, 0] + squared[:, 1]).reshape(blocks * 8, BLOCK)
        size = jnp.abs(sized).reshape(blocks, 2, 8, BLOCK)
        size = jnp.maximum(size[:, 0], size[:, 1]).reshape(blocks * 8, BLOCK)
        if g:
            squared = squares[...] + squared
            size = jnp.maximum(peaks[...], size)
        squares[...] = squared
        peaks[...] = size

    for g in range(groups):
        prepare(g)
        arrive(g)
    for g in range(groups):
        front(g)
        back(g)

    total = squares[pl.ds(0, blocks, stride=8), :]
    peak = jnp.maximum(peaks[pl.ds(0, blocks, stride=8), :], TINY)
    for row in range(1, 8):
        total = total + squares[pl.ds(row, blocks, stride=8), :]
        peak = jnp.maximum(peak, peaks[pl.ds(row, blocks, stride=8), :])
    exponent = jnp.ceil(jnp.log2(peak))
    inverses[...] = jnp.exp2(-exponent)
    square_out[...] = total
    for n in range(blocks):
        times = jnp.broadcast_to(inverses[pl.ds(n, 1), :], (WIDTH, BLOCK))
        for g in range(groups):
            part = gained[g, pl.ds(n * WIDTH, WIDTH), :] * times
            row = (n % 2) * local + g * WIDTH
            coded_out[n // 2, row : row + WIDTH, :] = part * jnp.abs(part) * TOP
    owners = blocks // 2
    coded_out[:, 2 * local : 2 * local + 2, :] = exponent.reshape(owners, 2, BLOCK)
    coded_out[:, 2 * local + 2 :, :] = jnp.zeros((owners, 6, BLOCK), jnp.float32)


def mix(place, streams, short_taps, rates, residues, skip, gain):
    channels, length = streams.shape[1:]
    blocks = length // BLOCK
    groups = channels // WIDTH
    rows = blocks * WIDTH
    short_taps = short_taps.transpose(0, 2, 1)
    rates = rates.T
    residues = residues.T
    skip = skip.reshape(-1, BLOCK)
    gain = gain.reshape(-1, BLOCK)
    shape = (blocks // 2, 2 * channels + 8, BLOCK)
    inputs = (streams, short_taps, rates, residues, skip, gain)
    return pl.pallas_call(
        mix_kernel,
        name="mix",
        grid_spec=pltpu.PrefetchScalarGridSpec(
            num_scalar_prefetch=1,
            grid=(1,),
            in_specs=[pl.BlockSpec(memory_space=pltpu.HBM)] * len(inputs),
            out_specs=[
                pl.BlockSpec(shape, lambda g, place: (0, 0, 0)),
                pl.BlockSpec((blocks, BLOCK), lambda g, place: (0, 0)),
            ],
            scratch_shapes=[
                *(pltpu.VMEM(array.shape, array.dtype) for array in inputs[1:]),
                pltpu.VMEM(streams.shape, jnp.bfloat16),
                pltpu.SemaphoreType.DMA((3 * groups + 5,)),
                pltpu.VMEM((groups, 3, 2 * BLOCK, 2 * BLOCK), jnp.bfloat16),
                pltpu.VMEM((groups, 2 * BLOCK, 4 * BLOCK), jnp.bfloat16),
                pltpu.VMEM((groups, BLOCK, BLOCK), jnp.bfloat16),
                pltpu.VMEM((groups, rows, BLOCK), jnp.float32),
                pltpu.VMEM((groups, rows, BLOCK), jnp.float32),
                pltpu.VMEM((groups, rows, BLOCK), jnp.float32),
                pltpu.VMEM((groups, rows, BLOCK), jnp.bfloat16),
                pltpu.VMEM((blocks * 8, BLOCK), jnp.float32),
                pltpu.VMEM((blocks * 8, BLOCK), jnp.float32),
                pltpu.VMEM((groups, rows, BLOCK), jnp.float32),
                pltpu.VMEM((blocks, BLOCK), jnp.float32),
            ],
        ),
        out_shape=[
            jax.ShapeDtypeStruct(shape, jnp.float32),
            jax.ShapeDtypeStruct((blocks, BLOCK), jnp.float32),
        ],
        compiler_params=pltpu.CompilerParams(
            dimension_semantics=("arbitrary",), vmem_limit_bytes=28 * 1024 * 1024
        ),
    )(
        place,
        *(
            pltpu.with_memory_space_constraint(array, pltpu.HBM)
            for array in inputs
        ),
    )


def finish_kernel(coded, mean_square, out):
    local = (coded.shape[1] - 8) // 2
    inverse_root = TOP**-0.5 * lax.rsqrt(mean_square[...] + 1e-05)
    for k in range(coded.shape[0]):
        times = jnp.exp2(coded[k, 2 * local : 2 * local + 2, :]) * inverse_root
        for h in range(2):
            value = coded[k, h * local : (h + 1) * local, :]
            root = value * lax.rsqrt(jnp.maximum(jnp.abs(value), 1e-20))
            out[k * local : (k + 1) * local, h * BLOCK : (h + 1) * BLOCK] = (
                root * jnp.broadcast_to(times[h : h + 1], value.shape)
            ).astype(jnp.bfloat16)


def finish(coded, mean_square, channels):
    owners, rows = coded.shape[:2]
    return pl.pallas_call(
        finish_kernel,
        name="finish",
        grid=(owners // AT_ONCE,),
        in_specs=[
            pl.BlockSpec((AT_ONCE, rows, BLOCK), lambda i: (i, 0, 0)),
            pl.BlockSpec((2, BLOCK), lambda i: (0, 0)),
        ],
        out_specs=pl.BlockSpec((AT_ONCE * channels, 2 * BLOCK), lambda i: (i, 0)),
        out_shape=jax.ShapeDtypeStruct((owners * channels, 2 * BLOCK), jnp.bfloat16),
        compiler_params=pltpu.CompilerParams(
            dimension_semantics=("arbitrary",), vmem_limit_bytes=12 * 1024 * 1024
        ),
    )(coded, mean_square)


def scattered(pieces, axis):
    count = lax.axis_size(axis)
    twice = jnp.concatenate([pieces, pieces], axis=0)
    turned = lax.dynamic_slice_in_dim(twice, lax.axis_index(axis), count, 0)
    total = turned[0]
    for by in range(1, count):
        pairs = [(i, (i + by) % count) for i in range(count)]
        total = total + lax.ppermute(turned[by], axis, pairs)
    return total


def with_partner(array, axis, bit):
    pairs = [(i, i ^ bit) for i in range(lax.axis_size(axis))]
    return array + lax.ppermute(array, axis, pairs)


def summed_for_owner(squares):
    z, x, core = (lax.axis_size(axis) for axis in CTX)
    squares = squares.reshape(z, x, core, 2, BLOCK).transpose(2, 1, 0, 3, 4)
    for axis in reversed(CTX):
        squares = scattered(squares, axis)
    return squares


def shards(streams, short_taps, pole_rates, residues, skip, gain):
    channels = streams.shape[1]
    place = lax.axis_index(CTX)
    coded, squares = mix(
        place.reshape(1), streams, short_taps, pole_rates, residues, skip, gain
    )
    squares = with_partner(squares, "ch", 1)
    moved = lax.all_to_all(coded.astype(jnp.float16), CTX, 0, 0, tiled=True)
    mean_square = summed_for_owner(with_partner(squares, "ch", 2)) / D
    return finish(moved.astype(jnp.float32), mean_square, channels)


def solution(mesh):
    torus = Mesh(mesh.devices.reshape(8, 4, 2, mesh.shape["ch"]), ("ctx_0", "ctx_1", "ctx_2", "ch"))
    in_specs = (
        P(None, CH_CTX, None),
        P(None, "ch", None),
        P("ch", None),
        P("ch", None),
        P("ch"),
        P("ch"),
    )
    out_specs = P("ch", CTX)
    return jax.shard_map(
        shards, mesh=torus, in_specs=in_specs, out_specs=out_specs, check_vma=False
    )
```
